512 devices in a mesh: row: 16 (over z), col: 16 (over y, x_lo, core), rep: 2 (over x_hi).
Axes of the slice: x: 4 (x_hi: 2, x_lo: 2; x = x_hi * 2 + x_lo), y: 4, z: 16, core: 2. Of those that a mesh axis runs over, the one named last changes fastest.
Arguments:
- tokens: bfloat16 [8192, 8192], P(('row', 'rep'), 'col'), may hold values from -6 to 6
- output_gradient: bfloat16 [8192, 8192], P(('row', 'rep'), 'col'), may hold values from -0.15625 to 0.15625
- master_weight: float32 [8192, 8192], P('row', 'col'), may hold values from -0.0625 to 0.0625
- old_down: float32 [8192, 128], P('row'), may hold values from -0.0625 to 0.0625
- old_up: float32 [128, 8192], P(None, 'col'), may hold values from -5 to 5
- fresh_down: float32 [8192, 128], P('col'), may hold values from -0.0625 to 0.0625
- fresh_up: float32 [128, 8192], P(None, 'col'), may hold values from -0.5 to 0.5
- m_down: float32 [8192, 128], P(('col', 'row')), may hold values from -6 to 6
- v_down: float32 [8192, 128], P(('col', 'row')), may hold values from 1 to 16
- m_up: float32 [128, 8192], P(None, ('col', 'row')), may hold values from -4 to 4
- v_up: float32 [128, 8192], P(None, ('col', 'row')), may hold values from 0.015625 to 0.25
- keep_down: int32 [512], P(('col', 'row')), may hold values 0 or 1
- keep_up: int32 [512], P(('col', 'row')), may hold values 0 or 1
Outputs:
- merged_weight: float32 [8192, 8192], P('row', 'col')
- w_copy: bfloat16 [8192, 8192], P('row', 'col')
- outputs: bfloat16 [8192, 8192], P(('row', 'rep'), 'col')
- m_down_new: float32 [8192, 128], P(('col', 'row'))
- v_down_new: float32 [8192, 128], P(('col', 'row'))
- m_up_new: float32 [128, 8192], P(None, ('col', 'row'))
- v_up_new: float32 [128, 8192], P(None, ('col', 'row'))
The draws below stay inside these ranges and needn't reach their ends.
All inputs are finite; a program needn't handle non-finite values. No bound on the sum of `keep_down` or of `keep_up` on one device may be relied on, other than what follows from the above.
Results may differ from the reference program's by a relative error of at most 0.0051.
Values may be sent and summed in bfloat16 or wider, within the bound.
A program may use at most 64 MiB of HBM per device.

```python
import math
import jax
import jax.numpy as jnp
from jax import lax

D = 8192
R = 128
BLOCK = 16
TOKENS = 8192


def place_ends(result, key, low, largest):
    longest = result.shape.index(max(result.shape))
    spots = []
    for shift in (0, 1):
        where = [jax.random.randint(jax.random.fold_in(key, axis), (), 0, length) for axis, length in enumerate(result.shape)]
        where[longest] = (where[longest] + shift) % result.shape[longest]
        spots.append(tuple(where))
    return result.at[spots[0]].set(low).at[spots[1]].set(largest)


def levels(stream_key, extent, shards, least, largest):
    def one(dim, parts):
        steps = jax.random.uniform(jax.random.fold_in(jax.random.fold_in(stream_key, 6), dim), (parts,), jnp.float32, least / len(shards), largest / len(shards))
        return jnp.repeat(jnp.exp(steps), extent[dim] // parts).reshape((-1,) + (1,) * (len(extent) - dim - 1))

    loudness = one(*shards[0])
    for cut in shards[1:]:
        loudness = loudness * one(*cut)
    return loudness


def noise(stream_key, extent, scale, bound, shards=(), dtype=jnp.bfloat16):
    values = scale * jax.random.normal(stream_key, extent, jnp.float32)
    if shards:
        values = values * levels(stream_key, extent, shards, -0.22, 0.18)
    return jnp.clip(values, -bound, bound).astype(dtype)


def setup_inputs(seed: int = 0) -> dict:
    key_list = jax.random.split(jax.random.key(seed), 14)
    return {
        "tokens": noise(key_list[0], (TOKENS, D), 1.0, 6.0, ((0, 32), (1, 16))),
        "output_gradient": noise(key_list[1], (TOKENS, D), (TOKENS ** -0.5), 0.15625, ((0, 32), (1, 16))),
        "master_weight": noise(key_list[2], (D, D), D ** -0.5, 0.0625, ((0, 16), (1, 16)), jnp.float32),
        "old_down": noise(key_list[3], (D, R), D ** -0.5, 0.0625, ((0, 16),), jnp.float32),
        "old_up": noise(key_list[4], (R, D), (4 * R ** -0.5), 5.0, ((1, 16),), jnp.float32),
        "fresh_down": noise(key_list[5], (D, R), D ** -0.5, 0.0625, ((0, 16),), jnp.float32),
        "fresh_up": noise(key_list[6], (R, D), R ** -0.5, 0.5, ((1, 16),), jnp.float32),
        "m_down": noise(key_list[7], (D, R), 2.0, 6.0, ((0, 256),), jnp.float32),
        "v_down": jnp.clip(jnp.exp(math.log(16.0) - 2.7725887 * jax.random.uniform(key_list[8], (D, R), jnp.float32) ** levels(key_list[8], (D, R), ((0, 256),), -0.2, 0.2)), 1.0, 16.0),
        "m_up": noise(key_list[9], (R, D), 0.25, 4.0, ((1, 256),), jnp.float32),
        "v_up": jnp.clip(jnp.exp(math.log(0.25) - 2.7725887 * jax.random.uniform(key_list[10], (R, D), jnp.float32) ** levels(key_list[10], (R, D), ((1, 256),), -0.2, 0.2)), 0.015625, 0.25),
        "keep_down": place_ends((jax.random.randint(key_list[11], (D // BLOCK,), 0, 4) < 3).astype(jnp.int32), jax.random.fold_in(key_list[11], 1), 0, 1),
        "keep_up": place_ends((jax.random.randint(key_list[12], (D // BLOCK,), 0, 4) < 3).astype(jnp.int32), jax.random.fold_in(key_list[12], 1), 0, 1),
    }


adapter_scale = 0.25
beta_one = 0.9
beta_two = 0.95


def reference(tokens, output_gradient, master_weight, old_down, old_up, fresh_down, fresh_up, m_down, v_down, m_up, v_up, keep_down, keep_up):
    previous_product = jnp.dot(old_down, old_up, precision=lax.Precision.HIGHEST, preferred_element_type=jnp.float32)
    merged_weight = master_weight + adapter_scale * previous_product
    w_copy = merged_weight.astype(jnp.bfloat16)
    down_cast = fresh_down.astype(jnp.bfloat16)
    up_cast = fresh_up.astype(jnp.bfloat16)
    hidden_rows = jnp.dot(tokens, down_cast, preferred_element_type=jnp.float32).astype(jnp.bfloat16)
    adapter_product = jnp.dot(tokens, w_copy, preferred_element_type=jnp.float32)
    adapter_branch = jnp.dot(hidden_rows, up_cast, preferred_element_type=jnp.float32)
    outputs = (adapter_product + adapter_scale * adapter_branch).astype(jnp.bfloat16)
    backward_pass = jnp.dot(output_gradient, up_cast.T, preferred_element_type=jnp.float32).astype(jnp.bfloat16)
    down_gradient = adapter_scale * jnp.dot(tokens.T, backward_pass, preferred_element_type=jnp.float32)
    up_gradient = adapter_scale * jnp.dot(hidden_rows.T, output_gradient, preferred_element_type=jnp.float32)
    keep_rows = jnp.repeat(keep_down.astype(jnp.float32), BLOCK)[:, None]
    keep_cols = jnp.repeat(keep_up.astype(jnp.float32), BLOCK)[None, :]
    m_down_new = beta_one * keep_rows * m_down + (1.0 - beta_one) * down_gradient
    v_down_new = beta_two * keep_rows * v_down + (1.0 - beta_two) * down_gradient * down_gradient
    m_up_new = beta_one * keep_cols * m_up + (1.0 - beta_one) * up_gradient
    v_up_new = beta_two * keep_cols * v_up + (1.0 - beta_two) * up_gradient * up_gradient
    return (merged_weight, w_copy, outputs, m_down_new, v_down_new, m_up_new, v_up_new)
```

```python
import jax
import jax.numpy as jnp
from jax import lax
from jax.experimental import pallas as pl
from jax.experimental.pallas import tpu as pltpu
from jax.sharding import PartitionSpec as P

BLOCK = 16
adapter_scale = 0.25
beta_one = 0.9
beta_two = 0.95

MESH = pl.DeviceIdType.MESH
NZ = 16
NC = 16
F32 = jnp.float32
BF16 = jnp.bfloat16


def split3(lhs, rhs):
    lhs_hi = lhs.astype(BF16)
    lhs_lo = (lhs - lhs_hi.astype(F32)).astype(BF16)
    rhs_hi = rhs.astype(BF16)
    rhs_lo = (rhs - rhs_hi.astype(F32)).astype(BF16)
    dot = lambda a, b: jnp.dot(a, b, preferred_element_type=F32)
    return dot(lhs_hi, rhs_hi) + (dot(lhs_hi, rhs_lo) + dot(lhs_lo, rhs_hi))


def contract_rows(lhs, rhs):
    return lax.dot_general(lhs, rhs, (((0,), (0,)), ((), ())), preferred_element_type=F32)


def kernel(
    tok, og, master, od, ou, fd, fu,
    merged, w, out, g,
    a_all, b_all, og_all, master_v, merged_v, w_v, od_v, ou_v, fd_v, fu_v,
    part, rs, hb_all, gtmp, gsend, grecv, gbuf, acc, stage,
    ld_sem, st_sem, b_send, b_recv, x_recv, y_recv, c_recv, a_send,
    rs_send, rs_recv, hb_send, hb_recv, og_sem, g_send, g_recv, gx_sem, o_send, o_recv,
):
    z = lax.axis_index("row")
    c = lax.axis_index("col")
    h = lax.axis_index("rep")
    other = 1 - h
    y = lax.div(c, 4)
    lo = lax.rem(lax.div(c, 2), 2)
    core = lax.rem(c, 2)
    px = 2 * h + lo
    me = h * NC + c

    def ring(d):
        return (lax.rem(z + (d + NZ), NZ), c, h)

    def plane(j):
        return (z, lax.rem(j, NC), lax.div(j, NC))

    def slot(xr, yr):
        pos = lax.rem(px + xr, 4)
        return lax.div(pos, 2) * NC + lax.rem(y + yr, 4) * 4 + lax.rem(pos, 2) * 2 + core

    def x_dev(xr):
        return plane(slot(xr, 0))

    def y_dev(yr):
        return plane(slot(0, yr))

    partner_core = (z, c + 1 - 2 * core, h)
    partner_rep = (z, c, other)

    def send(src, dst, send_sem, recv_sem, device):
        pltpu.make_async_remote_copy(
            src_ref=src, dst_ref=dst, send_sem=send_sem, recv_sem=recv_sem,
            device_id=device, device_id_type=MESH,
        ).start()

    def arrived(ref, sem):
        pltpu.make_async_remote_copy(
            src_ref=ref, dst_ref=ref, send_sem=a_send, recv_sem=sem,
            device_id=partner_core, device_id_type=MESH,
        ).wait_recv()

    def sent(ref, sem):
        pltpu.make_async_remote_copy(
            src_ref=ref, dst_ref=ref, send_sem=sem, recv_sem=a_send,
            device_id=partner_core, device_id_type=MESH,
        ).wait_send()

    loads = [
        pltpu.make_async_copy(src, dst, ld_sem.at[i])
        for i, (src, dst) in enumerate(
            [(od, od_v), (ou, ou_v), (master, master_v), (tok, a_all.at[me]), (fd, fd_v),
             (og, og_all.at[h]), (fu, fu_v)]
        )
    ]
    for load in loads:
        load.start()
    barrier = pltpu.get_barrier_semaphore()

    def greet_plane(d, carry):
        pl.semaphore_signal(barrier, inc=1, device_id=plane(lax.rem(me + d, 2 * NC)), device_id_type=MESH)
        return carry

    def greet_ring(d, carry):
        pl.semaphore_signal(barrier, inc=1, device_id=ring(d), device_id_type=MESH)
        return carry

    lax.fori_loop(1, 2 * NC, greet_plane, 0)
    lax.fori_loop(1, NZ, greet_ring, 0)

    for load in loads[:3]:
        load.wait()

    def merge(half):
        cols = pl.ds(pl.multiple_of(half * 256, 256), 256)
        both = master_v[:, cols] + adapter_scale * split3(od_v[...], ou_v[:, cols])
        merged_v[:, cols] = both
        w_v[:, cols] = both.astype(BF16)
        return both.astype(BF16)

    b_all[z] = merge(h)

    for load in loads[3:]:
        load.wait()
    down_cast = fd_v[...].astype(BF16)
    up_cast = fu_v[...].astype(BF16)
    hidden = jnp.dot(a_all[me], down_cast, preferred_element_type=F32)
    part[:, :, 0:128] = hidden.reshape(NC, 16, 128)
    backward = lax.dot_general(
        og_all[h], up_cast, (((1,), (1,)), ((), ())), preferred_element_type=F32
    )
    part[:, :, 128:256] = backward.reshape(NC, 16, 128)
    merge(other)
    stores = [
        pltpu.make_async_copy(merged_v, merged, st_sem.at[0]),
        pltpu.make_async_copy(w_v, w, st_sem.at[1]),
    ]
    for store in stores:
        store.start()

    pl.semaphore_wait(barrier, 2 * NC - 1 + NZ - 1)

    def chunk(zz, q):
        return b_all.at[zz, pl.ds((q % 2) * 256, 256), pl.ds((q // 2) * 128, 128)]

    def b_out(direction, step, q):
        sign = 1 if direction == 0 else -1
        origin = ring(-sign * (step - 1))[0]
        send(chunk(origin, q), chunk(origin, q), b_send, b_recv.at[direction, step - 1, q], ring(sign))

    def b_in(direction, step, q):
        sign = 1 if direction == 0 else -1
        origin = ring(-sign * step)[0]
        arrived(chunk(origin, q), b_recv.at[direction, step - 1, q])

    for q in range(4):
        for direction in (0, 1):
            b_out(direction, 1, q)

    def rs_out(d, carry):
        to = lax.rem(c + d, NC)
        send(part.at[to], rs.at[d - 1], rs_send, rs_recv, (z, to, h))
        return carry

    lax.fori_loop(1, NC, rs_out, 0)

    def a_out(at, recv_sem, device):
        send(a_all.at[at], a_all.at[at], a_send, recv_sem, device)

    forward = lax.select(core == 0, 3, 1)
    onward = lax.select(core == 0, 1, 3)

    def x_own():
        a_out(me, x_recv.at[3], x_dev(1))
        a_out(me, x_recv.at[1], x_dev(3))

    def x_in(xr):
        arrived(a_all.at[slot(xr, 0)], x_recv.at[xr])

    def x_forward():
        a_out(slot(forward, 0), x_recv.at[2], x_dev(onward))

    def core_out(xr, yr):
        a_out(slot(xr, yr), c_recv.at[xr], partner_core)

    def y_own(xr):
        a_out(slot(xr, 0), y_recv.at[xr, 3], y_dev(1))
        a_out(slot(xr, 0), y_recv.at[xr, 1], y_dev(3))

    def y_in(xr, yr):
        arrived(a_all.at[slot(xr, yr)], y_recv.at[xr, yr])

    def y_forward(xr):
        a_out(slot(xr, forward), y_recv.at[xr, 2], y_dev(onward))

    x_own()
    y_own(0)
    core_out(0, 0)
    send(og_all.at[h], og_all.at[h], og_sem.at[0], og_sem.at[1], partner_rep)

    def sum_rows():
        arrived(rs, rs_recv)
        total = part[c]
        for d in range(NC - 1):
            total = total + rs[d]
        hb_all[me] = total.astype(BF16)

        def hb_out(d, carry):
            send(hb_all.at[me], hb_all.at[me], hb_send, hb_recv, plane(lax.rem(me + d, 2 * NC)))
            return carry

        lax.fori_loop(1, 2 * NC, hb_out, 0)

    def rows_of(hp):
        return hb_all[pl.ds(hp * NC, NC)].reshape(256, 256)

    def start_outputs():
        arrived(hb_all.at[pl.ds(0, 2 * NC - 1)], hb_recv)
        cols = pl.ds(pl.multiple_of(h * 256, 256), 256)
        up_half = fu_v[:, cols].astype(BF16)
        for hp in (0, 1):
            acc[hp] = adapter_scale * jnp.dot(rows_of(hp)[:, :128], up_half, preferred_element_type=F32)

    def gradients():
        arrived(og_all.at[other], og_sem.at[1])
        down = jnp.zeros((512, 128), F32)
        up = jnp.zeros((512, 128), F32)
        for hp in (0, 1):
            rows = rows_of(hp)
            down = down + contract_rows(a_all[hp * NC + c], rows[:, 128:])
            up = up + contract_rows(og_all[hp], rows[:, :128])
        gtmp[0] = (adapter_scale * down).reshape(NZ, 2, 16, 128)
        gtmp[1] = (adapter_scale * up).reshape(NZ, 2, 16, 128)
        for u in (0, 1):
            gsend[:, u] = gtmp[u, :, h].astype(BF16)

        def g_out(d, carry):
            to = lax.rem(z + d, NZ)
            send(gsend.at[to], grecv.at[d - 1], g_send, g_recv, (to, c, h))
            return carry

        lax.fori_loop(1, NZ, g_out, 0)

    def sum_gradients():
        arrived(grecv, g_recv)
        for u in (0, 1):
            total = gtmp[u, z, h]
            for d in range(NZ - 1):
                total = total + grecv[d, u].astype(F32)
            gbuf[h, u] = total
        send(gbuf.at[h], gbuf.at[h], gx_sem.at[0], gx_sem.at[1], partner_rep)

    def end_gradients():
        arrived(gbuf.at[other], gx_sem.at[1])
        g[...] = gbuf[...]

    def product(zz):
        def one(hp, carry):
            acc[hp] += jnp.dot(a_all[hp * NC + zz], b_all[zz], preferred_element_type=F32)
            return carry

        lax.fori_loop(0, 2, one, 0)

    def products(first, last):
        def one(s, carry):
            product(lax.rem(z + s, NZ))
            product(lax.rem(z + (NZ - s), NZ))
            return carry

        lax.fori_loop(first, last + 1, one, 0)

    def first_products():
        for xr in (0, 3, 1, 2):
            arrived(a_all.at[pl.ds(0, 4)], c_recv.at[xr])
        product(z)
        products(1, 4)

    def x_near():
        for xr in (3, 1):
            x_in(xr)
        x_forward()
        for xr in (3, 1):
            core_out(xr, 0)

    def x_far():
        x_in(2)
        y_own(2)
        core_out(2, 0)

    def y_near(xr):
        y_in(xr, 3)
        y_in(xr, 1)
        y_forward(xr)
        core_out(xr, 3)
        core_out(xr, 1)

    def y_far(xr):
        y_in(xr, 2)
        core_out(xr, 2)

    after = {
        1: [sum_rows],
        3: [x_near, lambda: (y_own(3), y_own(1))],
        5: [start_outputs, lambda: y_near(0)],
        6: [x_far],
        7: [gradients],
        9: [lambda: y_far(0)],
        13: [lambda: y_near(3)],
        15: [lambda: y_near(1)],
        16: [sum_gradients],
        17: [lambda: y_far(3)],
        18: [lambda: y_near(2)],
        20: [lambda: y_far(1), end_gradients],
        22: [lambda: y_far(2)],
        23: [first_products],
        24: [lambda: products(5, 5)],
        25: [lambda: products(6, 6)],
        27: [lambda: products(7, 7)],
    }
    for tick in range(28):
        step, q = tick // 4 + 1, tick % 4
        for direction in (0, 1):
            b_in(direction, step, q)
            if step < 7 or q % 2 == direction:
                b_out(direction, step + 1, q)
        for action in after.get(tick, ()):
            action()

    far = lax.rem(z + 8, NZ)
    outs = []
    for part_of in (0, 1):
        for direction in (0, 1):
            b_in(direction, 8, 2 * part_of + direction)
        cols = pl.ds(part_of * 128, 128)
        there = pl.ds(pl.multiple_of(h * 256 + part_of * 128, 128), 128)
        for hp in (other, h):
            total = acc[hp, :, cols] + jnp.dot(
                a_all[hp * NC + far], b_all[far, :, cols], preferred_element_type=F32
            )
            stage[hp, part_of] = total.astype(BF16)
            if hp is other:
                send(stage.at[other, part_of], out.at[:, there], o_send.at[part_of], o_recv.at[part_of], partner_rep)
            else:
                keep = pltpu.make_async_copy(stage.at[h, part_of], out.at[:, there], st_sem.at[2 + part_of])
                keep.start()
                stores.append(keep)

    for store in stores:
        store.wait()
    sent(a_all.at[pl.ds(0, 31)], a_send)
    sent(b_all.at[pl.ds(0, 15)], b_send)
    sent(rs, rs_send)
    sent(hb_all.at[pl.ds(0, 2 * NC - 1)], hb_send)
    sent(og_all.at[h], og_sem.at[0])
    sent(grecv, g_send)
    sent(gbuf.at[h], gx_sem.at[0])
    for part_of in (0, 1):
        sent(stage.at[other, part_of], o_send.at[part_of])
        there = pl.ds(pl.multiple_of(other * 256 + part_of * 128, 128), 128)
        arrived(out.at[:, there], o_recv.at[part_of])


def adam_moments(first_moment, second_moment, keep_scale, gradient):
    first_new = beta_one * keep_scale * first_moment + (1.0 - beta_one) * gradient
    second_new = beta_two * keep_scale * second_moment + (1.0 - beta_two) * gradient * gradient
    return (first_new, second_new)


def body(
    tokens, output_gradient, master_weight, old_down, old_up, fresh_down, fresh_up,
    m_down, v_down, m_up, v_up, keep_down, keep_up,
):
    dma = pltpu.SemaphoreType.DMA
    vmem = pltpu.VMEM
    merged_weight, w_copy, outputs, g = pl.pallas_call(
        kernel,
        out_shape=(
            jax.ShapeDtypeStruct((512, 512), F32),
            jax.ShapeDtypeStruct((512, 512), BF16),
            jax.ShapeDtypeStruct((256, 512), BF16),
            jax.ShapeDtypeStruct((2, 2, 16, 128), F32),
        ),
        in_specs=[pl.BlockSpec(memory_space=pl.ANY)] * 7,
        out_specs=(
            pl.BlockSpec(memory_space=pl.ANY),
            pl.BlockSpec(memory_space=pl.ANY),
            pl.BlockSpec(memory_space=pl.ANY),
            pl.BlockSpec(memory_space=pltpu.VMEM),
        ),
        scratch_shapes=[
            vmem((2 * NC, 256, 512), BF16),
            vmem((NZ, 512, 256), BF16),
            vmem((2, 256, 512), BF16),
            vmem((512, 512), F32),
            vmem((512, 512), F32),
            vmem((512, 512), BF16),
            vmem((512, 128), F32),
            vmem((128, 512), F32),
            vmem((512, 128), F32),
            vmem((128, 512), F32),
            vmem((NC, 16, 256), F32),
            vmem((NC - 1, 16, 256), F32),
            vmem((2 * NC, 16, 256), BF16),
            vmem((2, NZ, 2, 16, 128), F32),
            vmem((NZ, 2, 16, 128), BF16),
            vmem((NZ - 1, 2, 16, 128), BF16),
            vmem((2, 2, 16, 128), F32),
            vmem((2, 256, 256), F32),
            vmem((2, 2, 256, 128), BF16),
            dma((7,)),
            dma((4,)),
            dma,
            dma((2, 8, 4)),
            dma((4,)),
            dma((4, 4)),
            dma((4,)),
            dma,
            dma,
            dma,
            dma,
            dma,
            dma((2,)),
            dma,
            dma,
            dma((2,)),
            dma((2,)),
            dma((2,)),
        ],
        compiler_params=pltpu.CompilerParams(
            collective_id=0, has_side_effects=True, vmem_limit_bytes=48 * 1024 * 1024
        ),
        name="relora_step",
    )(tokens, output_gradient, master_weight, old_down, old_up, fresh_down, fresh_up)
    down_rows = g[:, 0].reshape(32, 128)
    up_rows = g[:, 1].reshape(32, 128)
    keep_rows = jnp.repeat(keep_down.astype(F32), BLOCK)[:, None]
    keep_cols = jnp.repeat(keep_up.astype(F32), BLOCK)[None, :]
    m_down_new, v_down_new = adam_moments(m_down, v_down, keep_rows, down_rows)
    m_up_new, v_up_new = adam_moments(m_up, v_up, keep_cols, up_rows.T)
    return (merged_weight, w_copy, outputs, m_down_new, v_down_new, m_up_new, v_up_new)


def solution(mesh):
    both = P(("row", "rep"), "col")
    tile = P("row", "col")
    down = P(("col", "row"), None)
    up = P(None, ("col", "row"))
    flags = P(("col", "row"))
    return jax.shard_map(
        body,
        mesh=mesh,
        in_specs=(
            both, both, tile, P("row", None), P(None, "col"), P("col", None), P(None, "col"),
            down, down, up, up, flags, flags,
        ),
        out_specs=(tile, tile, both, down, down, up, up),
        check_vma=False,
    )
```

```python
import jax
import jax.numpy as jnp
from jax import lax
from jax.experimental import pallas as pl
from jax.experimental.pallas import tpu as pltpu
from jax.sharding import PartitionSpec as P

BLOCK = 16
adapter_scale = 0.25
beta_one = 0.9
beta_two = 0.95

MESH = pl.DeviceIdType.MESH
NZ = 16
NC = 16
F32 = jnp.float32
BF16 = jnp.bfloat16


def split3(lhs, rhs):
    lhs_hi = lhs.astype(BF16)
    lhs_lo = (lhs - lhs_hi.astype(F32)).astype(BF16)
    rhs_hi = rhs.astype(BF16)
    rhs_lo = (rhs - rhs_hi.astype(F32)).astype(BF16)
    dot = lambda a, b: jnp.dot(a, b, preferred_element_type=F32)
    return dot(lhs_hi, rhs_hi) + (dot(lhs_hi, rhs_lo) + dot(lhs_lo, rhs_hi))


def contract_rows(lhs, rhs):
    return lax.dot_general(lhs, rhs, (((0,), (0,)), ((), ())), preferred_element_type=F32)


def kernel(
    tok, og, master, od, ou, fd, fu, md, vd, mu, vu, kd, ku,
    merged, w, out, moments,
    a_all, b_all, og_v, master_v, merged_v, w_v, moments_v, od_v, ou_v, fd_v, fu_v,
    part, rs, hb_all, gtmp, up_send, up_recv, gsum, gsend, grecv, gbuf, acc, stage, old_moments, flags,
    ld_sem, st_sem, b_send, b_recv, p1_recv, p2_recv, c_recv, a_send,
    rs_send, rs_recv, hb_send, hb_recv, up_sem, g_send, g_recv, gx_sem, o_send, o_recv, far_sem,
):
    z = lax.axis_index("row")
    c = lax.axis_index("col")
    h = lax.axis_index("rep")
    other = 1 - h
    y = lax.div(c, 4)
    lo = lax.rem(lax.div(c, 2), 2)
    core = lax.rem(c, 2)
    px = 2 * h + lo
    me = h * NC + c

    def ring(d):
        return (lax.rem(z + (d + NZ), NZ), c, h)

    def plane(j):
        return (z, lax.rem(j, NC), lax.div(j, NC))

    def slot(xr, yr):
        pos = lax.rem(px + xr, 4)
        return lax.div(pos, 2) * NC + lax.rem(y + yr, 4) * 4 + lax.rem(pos, 2) * 2 + core

    def x_dev(xr):
        return plane(slot(xr, 0))

    def y_dev(yr):
        return plane(slot(0, yr))

    partner_core = (z, c + 1 - 2 * core, h)
    partner_rep = (z, c, other)

    def send(src, dst, send_sem, recv_sem, device):
        pltpu.make_async_remote_copy(
            src_ref=src, dst_ref=dst, send_sem=send_sem, recv_sem=recv_sem,
            device_id=device, device_id_type=MESH,
        ).start()

    def arrived(ref, sem):
        pltpu.make_async_remote_copy(
            src_ref=ref, dst_ref=ref, send_sem=a_send, recv_sem=sem,
            device_id=partner_core, device_id_type=MESH,
        ).wait_recv()

    def sent(ref, sem):
        pltpu.make_async_remote_copy(
            src_ref=ref, dst_ref=ref, send_sem=sem, recv_sem=a_send,
            device_id=partner_core, device_id_type=MESH,
        ).wait_send()

    loads = [
        pltpu.make_async_copy(src, dst, ld_sem.at[i])
        for i, (src, dst) in enumerate(
            [(od, od_v), (ou, ou_v), (master, master_v), (tok, a_all.at[me]), (fd, fd_v),
             (og, og_v), (fu, fu_v), (md, old_moments.at[0]), (vd, old_moments.at[1]),
             (mu, old_moments.at[2]), (vu, old_moments.at[3]), (kd, flags.at[0]), (ku, flags.at[1])]
        )
    ]
    for load in loads:
        load.start()
    barrier = pltpu.get_barrier_semaphore()

    def greet_plane(d, carry):
        pl.semaphore_signal(barrier, inc=1, device_id=plane(lax.rem(me + d, 2 * NC)), device_id_type=MESH)
        return carry

    def greet_ring(d, carry):
        pl.semaphore_signal(barrier, inc=1, device_id=ring(d), device_id_type=MESH)
        return carry

    lax.fori_loop(1, 2 * NC, greet_plane, 0)
    greet_ring(1, 0)
    greet_ring(-1, 0)

    for load in loads[:3]:
        load.wait()

    def merge(half):
        cols = pl.ds(pl.multiple_of(half * 256, 256), 256)
        both = master_v[:, cols] + adapter_scale * split3(od_v[...], ou_v[:, cols])
        merged_v[:, cols] = both
        w_v[:, cols] = both.astype(BF16)
        return both.astype(BF16)

    b_all[z] = merge(h)

    for load in loads[3:7]:
        load.wait()
    down_cast = fd_v[...].astype(BF16)
    up_cast = fu_v[...].astype(BF16)
    hidden = jnp.dot(a_all[me], down_cast, preferred_element_type=F32)
    part[:, :, 0:128] = hidden.reshape(NC, 16, 128)
    backward = lax.dot_general(
        og_v[...], up_cast, (((1,), (1,)), ((), ())), preferred_element_type=F32
    )
    part[:, :, 128:256] = backward.reshape(NC, 16, 128)
    merge(other)
    stores = [
        pltpu.make_async_copy(merged_v, merged, st_sem.at[2]),
        pltpu.make_async_copy(w_v, w, st_sem.at[3]),
    ]
    for store in stores:
        store.start()

    pl.semaphore_wait(barrier, 2 * NC - 1 + 2)

    def tell(i, distance):
        for d in (distance, -distance):
            pl.semaphore_signal(far_sem.at[i], inc=1, device_id=ring(d), device_id_type=MESH)

    def told(i):
        pl.semaphore_wait(far_sem.at[i], 2)

    tell(0, 1)

    def chunk(zz, q):
        return b_all.at[zz, pl.ds((q % 2) * 256, 256), pl.ds((q // 2) * 128, 128)]

    def b_out(direction, step, q):
        sign = 1 if direction == 0 else -1
        origin = ring(-sign * (step - 1))[0]
        send(chunk(origin, q), chunk(origin, q), b_send, b_recv.at[direction, step - 1, q], ring(sign))

    def b_in(direction, step, q):
        sign = 1 if direction == 0 else -1
        origin = ring(-sign * step)[0]
        arrived(chunk(origin, q), b_recv.at[direction, step - 1, q])

    for q in range(4):
        for direction in (0, 1):
            b_out(direction, 1, q)

    def rs_out(d, carry):
        to = lax.rem(c + d, NC)
        send(part.at[to], rs.at[d - 1], rs_send, rs_recv, (z, to, h))
        return carry

    lax.fori_loop(1, NC, rs_out, 0)

    forward = lax.select(core == 0, 3, 1)
    onward = lax.select(core == 0, 1, 3)

    def at(half, r1, r2):
        return a_all.at[slot(r1, r2) if half == 0 else slot(r2, r1), pl.ds(half * 128, 128)]

    def along(axis, r):
        return x_dev(r) if axis == 0 else y_dev(r)

    def a_out(ref, recv_sem, device):
        send(ref, ref, a_send, recv_sem, device)

    def core_out(half, r1, r2):
        a_out(at(half, r1, r2), c_recv.at[half, r1], partner_core)

    def p1_own(half):
        for d in (1, 3):
            a_out(at(half, 0, 0), p1_recv.at[half, 4 - d], along(half, d))

    def p2_own(half, r1):
        for d in (1, 3):
            a_out(at(half, r1, 0), p2_recv.at[half, r1, 4 - d], along(1 - half, d))
        core_out(half, r1, 0)

    def p1_near():
        for half in (0, 1):
            for r in (3, 1):
                arrived(at(half, r, 0), p1_recv.at[half, r])
            a_out(at(half, forward, 0), p1_recv.at[half, 2], along(half, onward))
        for half in (0, 1):
            p2_own(half, 3)
            p2_own(half, 1)

    def p1_far():
        for half in (0, 1):
            arrived(at(half, 2, 0), p1_recv.at[half, 2])
            p2_own(half, 2)

    def p2_near(half, r1):
        for r in (3, 1):
            arrived(at(half, r1, r), p2_recv.at[half, r1, r])
        a_out(at(half, r1, forward), p2_recv.at[half, r1, 2], along(1 - half, onward))
        core_out(half, r1, 3)
        core_out(half, r1, 1)

    def p2_far(half, r1):
        arrived(at(half, r1, 2), p2_recv.at[half, r1, 2])
        core_out(half, r1, 2)

    for half in (0, 1):
        p1_own(half)
    for half in (0, 1):
        p2_own(half, 0)

    def sum_rows():
        arrived(rs, rs_recv)
        total = part[c]
        for d in range(NC - 1):
            total = total + rs[d]
        hb_all[me] = total.astype(BF16)

        def hb_out(d, carry):
            send(hb_all.at[me], hb_all.at[me], hb_send, hb_recv, plane(lax.rem(me + d, 2 * NC)))
            return carry

        lax.fori_loop(1, 2 * NC, hb_out, 0)

    def rows_of(hp):
        return hb_all[pl.ds(hp * NC, NC)].reshape(256, 256)

    def start_outputs():
        arrived(hb_all.at[pl.ds(0, 2 * NC - 1)], hb_recv)
        cols = pl.ds(pl.multiple_of(h * 256, 256), 256)
        up_half = fu_v[:, cols].astype(BF16)
        for hp in (0, 1):
            acc[hp] = adapter_scale * jnp.dot(rows_of(hp)[:, :128], up_half, preferred_element_type=F32)

    def up_gradient():
        up = contract_rows(og_v[...], hb_all[pl.ds(h * NC, NC)].reshape(256, 256)[:, :128])
        gtmp[...] = (adapter_scale * up).reshape(NZ, 2, 16, 128)
        up_send[...] = gtmp[:, other].astype(BF16)
        gsum[1] = gtmp[:, h]
        send(up_send, up_recv, up_sem.at[0], up_sem.at[1], partner_rep)

    def gradients():
        down = jnp.zeros((512, 128), F32)
        for hp in (0, 1):
            down = down + contract_rows(a_all[hp * NC + c], rows_of(hp)[:, 128:])
        gtmp[...] = (adapter_scale * down).reshape(NZ, 2, 16, 128)
        gsum[0] = gtmp[:, h]
        arrived(up_recv, up_sem.at[1])
        gsum[1] += up_recv[...].astype(F32)
        for u in (0, 1):
            gsend[:, u] = gsum[u].astype(BF16)
        told(2)

        def g_out(d, carry):
            to = lax.rem(z + d, NZ)
            send(gsend.at[to], grecv.at[d - 1], g_send, g_recv, (to, c, h))
            return carry

        lax.fori_loop(1, NZ, g_out, 0)

    def sum_gradients():
        arrived(grecv, g_recv)
        for u in (0, 1):
            total = gsum[u, z]
            for d in range(NZ - 1):
                total = total + grecv[d, u].astype(F32)
            gbuf[h, u] = total
        send(gbuf.at[h], gbuf.at[h], gx_sem.at[0], gx_sem.at[1], partner_rep)

    def end_gradients():
        arrived(gbuf.at[other], gx_sem.at[1])
        for load in loads[7:]:
            load.wait()
        for u in (0, 1):
            for hp in (0, 1):
                rows = pl.ds(hp * 16, 16)
                keep = flags[u, hp].astype(F32)
                gradient = gbuf[hp, u]
                moments_v[2 * u, rows, :] = (beta_one * keep) * old_moments[2 * u, rows, :] + (1.0 - beta_one) * gradient
                moments_v[2 * u + 1, rows, :] = (beta_two * keep) * old_moments[2 * u + 1, rows, :] + (
                    (1.0 - beta_two) * gradient * gradient
                )
        store = pltpu.make_async_copy(moments_v, moments, st_sem.at[4])
        store.start()
        stores.append(store)

    def product(zz):
        def one(hp, carry):
            acc[hp] += jnp.dot(a_all[hp * NC + zz], b_all[zz], preferred_element_type=F32)
            return carry

        lax.fori_loop(0, 2, one, 0)

    def products(first, last):
        def one(s, carry):
            product(lax.rem(z + s, NZ))
            product(lax.rem(z + (NZ - s), NZ))
            return carry

        lax.fori_loop(first, last + 1, one, 0)

    def first_products():
        for half in (0, 1):
            for r1 in range(4):
                arrived(a_all.at[pl.ds(0, 2)], c_recv.at[half, r1])
        product(z)
        products(1, 1)

    def doubling():
        told(0)
        tell(1, 2)

    def doubled():
        told(1)
        tell(2, 4)

    after = {
        0: [doubling],
        1: [sum_rows],
        2: [doubled],
        3: [p1_near],
        5: [p1_far, start_outputs, up_gradient],
        6: [lambda: p2_near(1, 0), lambda: p2_near(0, 0)],
        8: [lambda: p2_far(1, 0), lambda: p2_far(0, 0), gradients],
        10: [lambda: p2_near(0, 3), lambda: p2_near(1, 3)],
        11: [lambda: p2_near(0, 1), lambda: p2_near(1, 1)],
        12: [lambda: p2_near(0, 2), lambda: p2_near(1, 2)],
        14: [lambda: p2_far(0, 3), lambda: p2_far(1, 3)],
        15: [lambda: p2_far(0, 1), lambda: p2_far(1, 1)],
        16: [lambda: p2_far(0, 2), lambda: p2_far(1, 2)],
        17: [sum_gradients],
        19: [first_products],
        20: [lambda: products(2, 2), end_gradients],
        21: [lambda: products(3, 3)],
        22: [lambda: products(4, 4)],
        23: [lambda: products(5, 5)],
        24: [lambda: products(6, 6)],
        27: [lambda: products(7, 7)],
    }
    for tick in range(28):
        step, q = tick // 4 + 1, tick % 4
        for direction in (0, 1):
            b_in(direction, step, q)
            if step < 7 or q % 2 == direction:
                b_out(direction, step + 1, q)
        for action in after.get(tick, ()):
            action()

    far = lax.rem(z + 8, NZ)
    outs = []
    for part_of in (0, 1):
        for direction in (0, 1):
            b_in(direction, 8, 2 * part_of + direction)
        cols = pl.ds(part_of * 128, 128)
        there = pl.ds(pl.multiple_of(h * 256 + part_of * 128, 128), 128)
        for hp in (other, h):
            total = acc[hp, :, cols] + jnp.dot(
                a_all[hp * NC + far], b_all[far, :, cols], preferred_element_type=F32
            )
            stage[hp, part_of] = total.astype(BF16)
            if hp is other:
                send(stage.at[other, part_of], out.at[:, there], o_send.at[part_of], o_recv.at[part_of], partner_rep)
            else:
                keep = pltpu.make_async_copy(stage.at[h, part_of], out.at[:, there], st_sem.at[part_of])
                keep.start()
                stores.append(keep)

    for store in stores:
        store.wait()
    sent(a_all.at[pl.ds(0, 31)], a_send)
    sent(b_all.at[pl.ds(0, 15)], b_send)
    sent(rs, rs_send)
    sent(hb_all.at[pl.ds(0, 2 * NC - 1)], hb_send)
    sent(up_send, up_sem.at[0])
    sent(grecv, g_send)
    sent(gbuf.at[h], gx_sem.at[0])
    for part_of in (0, 1):
        sent(stage.at[other, part_of], o_send.at[part_of])
        there = pl.ds(pl.multiple_of(other * 256 + part_of * 128, 128), 128)
        arrived(out.at[:, there], o_recv.at[part_of])


def write_out(merged, w, out, moments, merged_to, w_to, out_to, md, vd, mu, vu, merged_v, w_v, out_v, moments_v, sem):
    loads, stores = [], []
    for src, mid, dst in ((merged, merged_v, merged_to), (w, w_v, w_to), (out, out_v, out_to)):
        half = src.shape[0] // 2
        for rows in (pl.ds(0, half), pl.ds(half, half)):
            loads.append(pltpu.make_async_copy(src.at[rows], mid.at[rows], sem.at[len(loads)]))
            stores.append([pltpu.make_async_copy(mid.at[rows], dst.at[rows], sem.at[7 + len(stores)])])
    loads.append(pltpu.make_async_copy(moments, moments_v, sem.at[6]))
    stores.append([pltpu.make_async_copy(moments_v.at[i], ref, sem.at[13 + i]) for i, ref in enumerate((md, vd, mu, vu))])
    for load in loads:
        load.start()
    for load, after in zip(loads, stores):
        load.wait()
        for store in after:
            store.start()
    for after in stores:
        for store in after:
            store.wait()


def body(
    tokens, output_gradient, master_weight, old_down, old_up, fresh_down, fresh_up,
    m_down, v_down, m_up, v_up, keep_down, keep_up,
):
    dma = pltpu.SemaphoreType.DMA
    vmem = pltpu.VMEM
    hbm = pl.BlockSpec(memory_space=pltpu.HBM)
    results = pl.pallas_call(
        kernel,
        out_shape=(
            jax.ShapeDtypeStruct((512, 512), F32),
            jax.ShapeDtypeStruct((512, 512), BF16),
            jax.ShapeDtypeStruct((256, 512), BF16),
            jax.ShapeDtypeStruct((4, 32, 128), F32),
        ),
        in_specs=[hbm] * 13,
        out_specs=(hbm,) * 4,
        scratch_shapes=[
            vmem((2 * NC, 256, 512), BF16),
            vmem((NZ, 512, 256), BF16),
            vmem((256, 512), BF16),
            vmem((512, 512), F32),
            vmem((512, 512), F32),
            vmem((512, 512), BF16),
            vmem((4, 32, 128), F32),
            vmem((512, 128), F32),
            vmem((128, 512), F32),
            vmem((512, 128), F32),
            vmem((128, 512), F32),
            vmem((NC, 16, 256), F32),
            vmem((NC - 1, 16, 256), F32),
            vmem((2 * NC, 16, 256), BF16),
            vmem((NZ, 2, 16, 128), F32),
            vmem((NZ, 16, 128), BF16),
            vmem((NZ, 16, 128), BF16),
            vmem((2, NZ, 16, 128), F32),
            vmem((NZ, 2, 16, 128), BF16),
            vmem((NZ - 1, 2, 16, 128), BF16),
            vmem((2, 2, 16, 128), F32),
            vmem((2, 256, 256), F32),
            vmem((2, 2, 256, 128), BF16),
            vmem((4, 32, 128), F32),
            pltpu.SMEM((2, 2), jnp.int32),
            dma((13,)),
            dma((5,)),
            dma,
            dma((2, 8, 4)),
            dma((2, 4)),
            dma((2, 4, 4)),
            dma((2, 4)),
            dma,
            dma,
            dma,
            dma,
            dma,
            dma((2,)),
            dma,
            dma,
            dma((2,)),
            dma((2,)),
            dma((2,)),
            pltpu.SemaphoreType.REGULAR((3,)),
        ],
        compiler_params=pltpu.CompilerParams(
            collective_id=0, has_side_effects=True, vmem_limit_bytes=60 * 1024 * 1024
        ),
        name="relora_step",
    )(
        tokens, output_gradient, master_weight, old_down, old_up, fresh_down, fresh_up,
        m_down, v_down, m_up.T, v_up.T, keep_down, keep_up,
    )
    small = jax.ShapeDtypeStruct((32, 128), F32)
    merged_weight, w_copy, outputs, md, vd, mu, vu = pl.pallas_call(
        write_out,
        out_shape=(
            jax.ShapeDtypeStruct((512, 512), F32),
            jax.ShapeDtypeStruct((512, 512), BF16),
            jax.ShapeDtypeStruct((256, 512), BF16),
            small, small, small, small,
        ),
        in_specs=[hbm] * 4,
        out_specs=(hbm,) * 7,
        scratch_shapes=[
            vmem((512, 512), F32), vmem((512, 512), BF16), vmem((256, 512), BF16), vmem((4, 32, 128), F32), dma((17,)),
        ],
        compiler_params=pltpu.CompilerParams(vmem_limit_bytes=60 * 1024 * 1024),
        name="write_out",
    )(*results)
    return (merged_weight, w_copy, outputs, md, vd, mu.T, vu.T)


def solution(mesh):
    both = P(("row", "rep"), "col")
    tile = P("row", "col")
    down = P(("col", "row"), None)
    up = P(None, ("col", "row"))
    flags = P(("col", "row"))
    return jax.shard_map(
        body,
        mesh=mesh,
        in_specs=(
            both, both, tile, P("row", None), P(None, "col"), P("col", None), P(None, "col"),
            down, down, up, up, flags, flags,
        ),
        out_specs=(tile, tile, both, down, down, up, up),
        check_vma=False,
    )
```

```python
import jax
import jax.numpy as jnp
from jax import lax
from jax.experimental import pallas as pl
from jax.experimental.pallas import tpu as pltpu
from jax.sharding import PartitionSpec as P

BLOCK = 16
adapter_scale = 0.25
beta_one = 0.9
beta_two = 0.95

MESH = pl.DeviceIdType.MESH
NZ = 16
NC = 16
F32 = jnp.float32
BF16 = jnp.bfloat16


def split3(lhs, rhs):
    lhs_hi = lhs.astype(BF16)
    lhs_lo = (lhs - lhs_hi.astype(F32)).astype(BF16)
    rhs_hi = rhs.astype(BF16)
    rhs_lo = (rhs - rhs_hi.astype(F32)).astype(BF16)
    dot = lambda a, b: jnp.dot(a, b, preferred_element_type=F32)
    return dot(lhs_hi, rhs_hi) + (dot(lhs_hi, rhs_lo) + dot(lhs_lo, rhs_hi))


def contract_rows(lhs, rhs):
    return lax.dot_general(lhs, rhs, (((0,), (0,)), ((), ())), preferred_element_type=F32)


def kernel(
    tok, og, master, od, ou, fd, fu, md, vd, mu, vu, kd, ku,
    merged, w, out, moments,
    a_all, b_all, og_v, master_v, merged_v, w_v, moments_v, od_v, ou_v, fd_v, fu_v,
    part, rs, hb_all, gtmp, up_send, up_recv, gsum, gsend, grecv, gbuf, acc, stage, old_moments, flags,
    ld_sem, st_sem, b_send, b_recv, p1_recv, p2_recv, c_recv, a_send,
    rs_send, rs_recv, hb_send, hb_recv, up_sem, g_send, g_recv, gx_sem, o_send, o_recv, far_sem,
):
    z = lax.axis_index("row")
    c = lax.axis_index("col")
    h = lax.axis_index("rep")
    other = 1 - h
    y = lax.div(c, 4)
    lo = lax.rem(lax.div(c, 2), 2)
    core = lax.rem(c, 2)
    px = 2 * h + lo
    me = h * NC + c

    def ring(d):
        return (lax.rem(z + (d + NZ), NZ), c, h)

    def plane(j):
        return (z, lax.rem(j, NC), lax.div(j, NC))

    def slot(xr, yr):
        pos = lax.rem(px + xr, 4)
        return lax.div(pos, 2) * NC + lax.rem(y + yr, 4) * 4 + lax.rem(pos, 2) * 2 + core

    def x_dev(xr):
        return plane(slot(xr, 0))

    def y_dev(yr):
        return plane(slot(0, yr))

    partner_core = (z, c + 1 - 2 * core, h)
    partner_rep = (z, c, other)

    def send(src, dst, send_sem, recv_sem, device):
        pltpu.make_async_remote_copy(
            src_ref=src, dst_ref=dst, send_sem=send_sem, recv_sem=recv_sem,
            device_id=device, device_id_type=MESH,
        ).start()

    def arrived(ref, sem):
        pltpu.make_async_remote_copy(
            src_ref=ref, dst_ref=ref, send_sem=a_send, recv_sem=sem,
            device_id=partner_core, device_id_type=MESH,
        ).wait_recv()

    def sent(ref, sem):
        pltpu.make_async_remote_copy(
            src_ref=ref, dst_ref=ref, send_sem=sem, recv_sem=a_send,
            device_id=partner_core, device_id_type=MESH,
        ).wait_send()

    def columns(half):
        return pl.ds(pl.multiple_of(half * 256, 256), 256)

    loads = [
        pltpu.make_async_copy(src, dst, ld_sem.at[i])
        for i, (src, dst) in enumerate(
            [(od, od_v), (ou, ou_v), (master.at[:, columns(h)], master_v.at[:, columns(h)]),
             (tok, a_all.at[me]), (fd, fd_v), (og, og_v), (fu, fu_v), (md, old_moments.at[0]), (vd, old_moments.at[1]),
             (mu, old_moments.at[2]), (vu, old_moments.at[3]), (kd, flags.at[0]), (ku, flags.at[1]),
             (master.at[:, columns(other)], master_v.at[:, columns(other)])]
        )
    ]
    for load in loads:
        load.start()
    barrier = pltpu.get_barrier_semaphore()
    for d in (1, -1):
        pl.semaphore_signal(barrier, inc=1, device_id=ring(d), device_id_type=MESH)

    def greet_plane(d, carry):
        pl.semaphore_signal(barrier, inc=1, device_id=plane(lax.rem(me + d, 2 * NC)), device_id_type=MESH)
        return carry

    lax.fori_loop(1, 2 * NC, greet_plane, 0)

    for load in loads[:3]:
        load.wait()

    def merge(half):
        cols = columns(half)
        both = master_v[:, cols] + adapter_scale * split3(od_v[...], ou_v[:, cols])
        merged_v[:, cols] = both
        w_v[:, cols] = both.astype(BF16)
        return both.astype(BF16)

    b_all[z] = merge(h)
    pl.semaphore_wait(barrier, 2 * NC - 1 + 2)

    def tell(i, distance):
        for d in (distance, -distance):
            pl.semaphore_signal(far_sem.at[i], inc=1, device_id=ring(d), device_id_type=MESH)

    def told(i):
        pl.semaphore_wait(far_sem.at[i], 2)

    def chunk(zz, q):
        return b_all.at[zz, pl.ds((q % 2) * 256, 256), pl.ds((q // 2) * 128, 128)]

    def b_out(direction, step, q):
        sign = 1 if direction == 0 else -1
        origin = ring(-sign * (step - 1))[0]
        send(chunk(origin, q), chunk(origin, q), b_send, b_recv.at[direction, step - 1, q], ring(sign))

    def b_in(direction, step, q):
        sign = 1 if direction == 0 else -1
        origin = ring(-sign * step)[0]
        arrived(chunk(origin, q), b_recv.at[direction, step - 1, q])

    for q in range(4):
        for direction in (0, 1):
            b_out(direction, 1, q)

    tell(0, 1)

    for load in loads[3:7]:
        load.wait()
    down_cast = fd_v[...].astype(BF16)
    up_cast = fu_v[...].astype(BF16)
    hidden = jnp.dot(a_all[me], down_cast, preferred_element_type=F32)
    part[:, :, 0:128] = hidden.reshape(NC, 16, 128)
    backward = lax.dot_general(
        og_v[...], up_cast, (((1,), (1,)), ((), ())), preferred_element_type=F32
    )
    part[:, :, 128:256] = backward.reshape(NC, 16, 128)

    def rs_out(d, carry):
        to = lax.rem(c + d, NC)
        send(part.at[to], rs.at[d - 1], rs_send, rs_recv, (z, to, h))
        return carry

    lax.fori_loop(1, NC, rs_out, 0)

    forward = lax.select(core == 0, 3, 1)
    onward = lax.select(core == 0, 1, 3)

    def at(half, r1, r2):
        return a_all.at[slot(r1, r2) if half == 0 else slot(r2, r1), pl.ds(half * 128, 128)]

    def along(axis, r):
        return x_dev(r) if axis == 0 else y_dev(r)

    def a_out(ref, recv_sem, device):
        send(ref, ref, a_send, recv_sem, device)

    def core_out(half, r1, r2):
        a_out(at(half, r1, r2), c_recv.at[half, r1], partner_core)

    def p1_own(half):
        for d in (1, 3):
            a_out(at(half, 0, 0), p1_recv.at[half, 4 - d], along(half, d))

    def p2_own(half, r1):
        for d in (1, 3):
            a_out(at(half, r1, 0), p2_recv.at[half, r1, 4 - d], along(1 - half, d))
        core_out(half, r1, 0)

    def p1_near():
        for half in (0, 1):
            for r in (3, 1):
                arrived(at(half, r, 0), p1_recv.at[half, r])
            a_out(at(half, forward, 0), p1_recv.at[half, 2], along(half, onward))
        for half in (0, 1):
            p2_own(half, 3)
            p2_own(half, 1)

    def p1_far():
        for half in (0, 1):
            arrived(at(half, 2, 0), p1_recv.at[half, 2])
            p2_own(half, 2)

    def p2_near(half, r1):
        for r in (3, 1):
            arrived(at(half, r1, r), p2_recv.at[half, r1, r])
        a_out(at(half, r1, forward), p2_recv.at[half, r1, 2], along(1 - half, onward))
        core_out(half, r1, 3)
        core_out(half, r1, 1)

    def p2_far(half, r1):
        arrived(at(half, r1, 2), p2_recv.at[half, r1, 2])
        core_out(half, r1, 2)

    for half in (0, 1):
        p1_own(half)
    for half in (0, 1):
        p2_own(half, 0)

    loads[13].wait()
    merge(other)
    stores = [
        pltpu.make_async_copy(merged_v, merged, st_sem.at[2]),
        pltpu.make_async_copy(w_v, w, st_sem.at[3]),
    ]
    for store in stores:
        store.start()

    def sum_rows():
        arrived(rs, rs_recv)
        total = part[c]
        for d in range(NC - 1):
            total = total + rs[d]
        hb_all[me] = total.astype(BF16)

        def hb_out(d, carry):
            send(hb_all.at[me], hb_all.at[me], hb_send, hb_recv, plane(lax.rem(me + d, 2 * NC)))
            return carry

        lax.fori_loop(1, 2 * NC, hb_out, 0)

    def rows_of(hp):
        return hb_all[pl.ds(hp * NC, NC)].reshape(256, 256)

    def start_outputs():
        arrived(hb_all.at[pl.ds(0, 2 * NC - 1)], hb_recv)
        up_half = fu_v[:, columns(h)].astype(BF16)
        for hp in (0, 1):
            acc[hp] = adapter_scale * jnp.dot(rows_of(hp)[:, :128], up_half, preferred_element_type=F32)

    def up_gradient():
        up = contract_rows(og_v[...], hb_all[pl.ds(h * NC, NC)].reshape(256, 256)[:, :128])
        gtmp[...] = (adapter_scale * up).reshape(NZ, 2, 16, 128)
        up_send[...] = gtmp[:, other].astype(BF16)
        gsum[1] = gtmp[:, h]
        send(up_send, up_recv, up_sem.at[0], up_sem.at[1], partner_rep)

    def gradients():
        down = jnp.zeros((512, 128), F32)
        for hp in (0, 1):
            down = down + contract_rows(a_all[hp * NC + c], rows_of(hp)[:, 128:])
        gtmp[...] = (adapter_scale * down).reshape(NZ, 2, 16, 128)
        gsum[0] = gtmp[:, h]
        arrived(up_recv, up_sem.at[1])
        gsum[1] += up_recv[...].astype(F32)
        for u in (0, 1):
            gsend[:, u] = gsum[u].astype(BF16)
        told(2)

        def g_out(d, carry):
            to = lax.rem(z + d, NZ)
            send(gsend.at[to], grecv.at[d - 1], g_send, g_recv, (to, c, h))
            return carry

        lax.fori_loop(1, NZ, g_out, 0)

    def sum_gradients():
        arrived(grecv, g_recv)
        for u in (0, 1):
            total = gsum[u, z]
            for d in range(NZ - 1):
                total = total + grecv[d, u].astype(F32)
            gbuf[h, u] = total
        send(gbuf.at[h], gbuf.at[h], gx_sem.at[0], gx_sem.at[1], partner_rep)

    def end_gradients():
        arrived(gbuf.at[other], gx_sem.at[1])
        for load in loads[7:13]:
            load.wait()
        for u in (0, 1):
            for hp in (0, 1):
                rows = pl.ds(hp * 16, 16)
                keep = flags[u, hp].astype(F32)
                gradient = gbuf[hp, u]
                moments_v[2 * u, rows, :] = (beta_one * keep) * old_moments[2 * u, rows, :] + (1.0 - beta_one) * gradient
                moments_v[2 * u + 1, rows, :] = (beta_two * keep) * old_moments[2 * u + 1, rows, :] + (
                    (1.0 - beta_two) * gradient * gradient
                )
        store = pltpu.make_async_copy(moments_v, moments, st_sem.at[4])
        store.start()
        stores.append(store)

    def product(zz):
        def one(hp, carry):
            acc[hp] += jnp.dot(a_all[hp * NC + zz], b_all[zz], preferred_element_type=F32)
            return carry

        lax.fori_loop(0, 2, one, 0)

    def products(first, last):
        def one(s, carry):
            product(lax.rem(z + s, NZ))
            product(lax.rem(z + (NZ - s), NZ))
            return carry

        lax.fori_loop(first, last + 1, one, 0)

    def first_products():
        for half in (0, 1):
            for r1 in range(4):
                arrived(a_all.at[pl.ds(0, 2)], c_recv.at[half, r1])
        product(z)
        products(1, 1)

    def doubling():
        told(0)
        tell(1, 2)

    def doubled():
        told(1)
        tell(2, 4)

    after = {
        0: [doubling],
        2: [doubled],
        3: [sum_rows],
        4: [p1_near],
        6: [lambda: p2_near(1, 0), lambda: p2_near(0, 0)],
        7: [p1_far],
        10: [start_outputs, up_gradient],
        11: [lambda: p2_near(0, 3), lambda: p2_near(1, 3)],
        12: [lambda: p2_near(0, 1), lambda: p2_near(1, 1), lambda: p2_far(1, 0)],
        13: [lambda: p2_far(0, 0)],
        14: [gradients],
        15: [lambda: p2_near(0, 2), lambda: p2_near(1, 2)],
        18: [lambda: p2_far(0, 3), lambda: p2_far(1, 3)],
        19: [lambda: p2_far(0, 1), lambda: p2_far(1, 1)],
        20: [lambda: p2_far(0, 2), lambda: p2_far(1, 2)],
        22: [first_products],
        23: [sum_gradients, lambda: products(2, 3)],
        24: [lambda: products(4, 5)],
        25: [lambda: products(6, 6)],
        27: [lambda: products(7, 7), end_gradients],
    }
    for tick in range(28):
        step, q = tick // 4 + 1, tick % 4
        for direction in (0, 1):
            b_in(direction, step, q)
            if step < 7 or q % 2 == direction:
                b_out(direction, step + 1, q)
        for action in after.get(tick, ()):
            action()

    far = lax.rem(z + 8, NZ)
    outs = []
    for part_of in (0, 1):
        for direction in (0, 1):
            b_in(direction, 8, 2 * part_of + direction)
        cols = pl.ds(part_of * 128, 128)
        there = pl.ds(pl.multiple_of(h * 256 + part_of * 128, 128), 128)
        for hp in (other, h):
            total = acc[hp, :, cols] + jnp.dot(
                a_all[hp * NC + far], b_all[far, :, cols], preferred_element_type=F32
            )
            stage[hp, part_of] = total.astype(BF16)
            if hp is other:
                send(stage.at[other, part_of], out.at[:, there], o_send.at[part_of], o_recv.at[part_of], partner_rep)
            else:
                keep = pltpu.make_async_copy(stage.at[h, part_of], out.at[:, there], st_sem.at[part_of])
                keep.start()
                stores.append(keep)

    for store in stores:
        store.wait()
    sent(a_all.at[pl.ds(0, 31)], a_send)
    sent(b_all.at[pl.ds(0, 15)], b_send)
    sent(rs, rs_send)
    sent(hb_all.at[pl.ds(0, 2 * NC - 1)], hb_send)
    sent(up_send, up_sem.at[0])
    sent(grecv, g_send)
    sent(gbuf.at[h], gx_sem.at[0])
    for part_of in (0, 1):
        sent(stage.at[other, part_of], o_send.at[part_of])
        there = pl.ds(pl.multiple_of(other * 256 + part_of * 128, 128), 128)
        arrived(out.at[:, there], o_recv.at[part_of])


def write_out(merged, w, out, moments, merged_to, w_to, out_to, md, vd, mu, vu, merged_v, w_v, out_v, moments_v, sem):
    loads, stores = [], []
    for src, mid, dst in ((merged, merged_v, merged_to), (w, w_v, w_to), (out, out_v, out_to)):
        half = src.shape[0] // 2
        for rows in (pl.ds(0, half), pl.ds(half, half)):
            loads.append(pltpu.make_async_copy(src.at[rows], mid.at[rows], sem.at[len(loads)]))
            stores.append([pltpu.make_async_copy(mid.at[rows], dst.at[rows], sem.at[7 + len(stores)])])
    loads.append(pltpu.make_async_copy(moments, moments_v, sem.at[6]))
    stores.append([pltpu.make_async_copy(moments_v.at[i], ref, sem.at[13 + i]) for i, ref in enumerate((md, vd, mu, vu))])
    for load in loads:
        load.start()
    for load, after in zip(loads, stores):
        load.wait()
        for store in after:
            store.start()
    for after in stores:
        for store in after:
            store.wait()


def body(
    tokens, output_gradient, master_weight, old_down, old_up, fresh_down, fresh_up,
    m_down, v_down, m_up, v_up, keep_down, keep_up,
):
    dma = pltpu.SemaphoreType.DMA
    vmem = pltpu.VMEM
    hbm = pl.BlockSpec(memory_space=pltpu.HBM)
    results = pl.pallas_call(
        kernel,
        out_shape=(
            jax.ShapeDtypeStruct((512, 512), F32),
            jax.ShapeDtypeStruct((512, 512), BF16),
            jax.ShapeDtypeStruct((256, 512), BF16),
            jax.ShapeDtypeStruct((4, 32, 128), F32),
        ),
        in_specs=[hbm] * 13,
        out_specs=(hbm,) * 4,
        scratch_shapes=[
            vmem((2 * NC, 256, 512), BF16),
            vmem((NZ, 512, 256), BF16),
            vmem((256, 512), BF16),
            vmem((512, 512), F32),
            vmem((512, 512), F32),
            vmem((512, 512), BF16),
            vmem((4, 32, 128), F32),
            vmem((512, 128), F32),
            vmem((128, 512), F32),
            vmem((512, 128), F32),
            vmem((128, 512), F32),
            vmem((NC, 16, 256), F32),
            vmem((NC - 1, 16, 256), F32),
            vmem((2 * NC, 16, 256), BF16),
            vmem((NZ, 2, 16, 128), F32),
            vmem((NZ, 16, 128), BF16),
            vmem((NZ, 16, 128), BF16),
            vmem((2, NZ, 16, 128), F32),
            vmem((NZ, 2, 16, 128), BF16),
            vmem((NZ - 1, 2, 16, 128), BF16),
            vmem((2, 2, 16, 128), F32),
            vmem((2, 256, 256), F32),
            vmem((2, 2, 256, 128), BF16),
            vmem((4, 32, 128), F32),
            pltpu.SMEM((2, 2), jnp.int32),
            dma((14,)),
            dma((5,)),
            dma,
            dma((2, 8, 4)),
            dma((2, 4)),
            dma((2, 4, 4)),
            dma((2, 4)),
            dma,
            dma,
            dma,
            dma,
            dma,
            dma((2,)),
            dma,
            dma,
            dma((2,)),
            dma((2,)),
            dma((2,)),
            pltpu.SemaphoreType.REGULAR((3,)),
        ],
        compiler_params=pltpu.CompilerParams(
            collective_id=0, has_side_effects=True, vmem_limit_bytes=60 * 1024 * 1024
        ),
        name="relora_step",
    )(
        tokens, output_gradient, master_weight, old_down, old_up, fresh_down, fresh_up,
        m_down, v_down, m_up.T, v_up.T, keep_down, keep_up,
    )
    small = jax.ShapeDtypeStruct((32, 128), F32)
    merged_weight, w_copy, outputs, md, vd, mu, vu = pl.pallas_call(
        write_out,
        out_shape=(
            jax.ShapeDtypeStruct((512, 512), F32),
            jax.ShapeDtypeStruct((512, 512), BF16),
            jax.ShapeDtypeStruct((256, 512), BF16),
            small, small, small, small,
        ),
        in_specs=[hbm] * 4,
        out_specs=(hbm,) * 7,
        scratch_shapes=[
            vmem((512, 512), F32), vmem((512, 512), BF16), vmem((256, 512), BF16), vmem((4, 32, 128), F32), dma((17,)),
        ],
        compiler_params=pltpu.CompilerParams(vmem_limit_bytes=60 * 1024 * 1024),
        name="write_out",
    )(*results)
    return (merged_weight, w_copy, outputs, md, vd, mu.T, vu.T)


def solution(mesh):
    both = P(("row", "rep"), "col")
    tile = P("row", "col")
    down = P(("col", "row"), None)
    up = P(None, ("col", "row"))
    flags = P(("col", "row"))
    return jax.shard_map(
        body,
        mesh=mesh,
        in_specs=(
            both, both, tile, P("row", None), P(None, "col"), P("col", None), P(None, "col"),
            down, down, up, up, flags, flags,
        ),
        out_specs=(tile, tile, both, down, down, up, up),
        check_vma=False,
    )
```

```python
import jax
import jax.numpy as jnp
from jax import lax
from jax.experimental import pallas as pl
from jax.experimental.pallas import tpu as pltpu
from jax.sharding import PartitionSpec as P

BLOCK = 16
adapter_scale = 0.25
beta_one = 0.9
beta_two = 0.95

MESH = pl.DeviceIdType.MESH
NZ = 16
NC = 16
F32 = jnp.float32
BF16 = jnp.bfloat16


def split3(lhs, rhs):
    lhs_hi = lhs.astype(BF16)
    lhs_lo = (lhs - lhs_hi.astype(F32)).astype(BF16)
    rhs_hi = rhs.astype(BF16)
    rhs_lo = (rhs - rhs_hi.astype(F32)).astype(BF16)
    dot = lambda a, b: jnp.dot(a, b, preferred_element_type=F32)
    return dot(lhs_hi, rhs_hi) + (dot(lhs_hi, rhs_lo) + dot(lhs_lo, rhs_hi))


def contract_rows(lhs, rhs):
    return lax.dot_general(lhs, rhs, (((0,), (0,)), ((), ())), preferred_element_type=F32)


def kernel(
    tok, og, master, od, ou, fd, fu, md, vd, mu, vu, kd, ku,
    merged, w, out, moments,
    a_all, b_all, og_v, master_v, merged_v, w_v, moments_v, od_v, ou_v, fd_v, fu_v,
    part, rs, hb_all, gtmp, up_send, up_recv, gsum, pair_send, pair_recv, gsend, grecv, gbuf, acc, stage, old_moments, flags,
    ld_sem, st_sem, b_send, b_recv, p1_recv, p2_recv, c_recv, a_send,
    rs_send, rs_recv, hb_send, hb_recv, up_sem, pair_sem, g_send, g_recv, gx_sem, o_send, o_recv, far_sem,
):
    z = lax.axis_index("row")
    c = lax.axis_index("col")
    h = lax.axis_index("rep")
    other = 1 - h
    y = lax.div(c, 4)
    lo = lax.rem(lax.div(c, 2), 2)
    core = lax.rem(c, 2)
    px = 2 * h + lo
    me = h * NC + c

    def ring(d):
        return (lax.rem(z + (d + NZ), NZ), c, h)

    def plane(j):
        return (z, lax.rem(j, NC), lax.div(j, NC))

    def slot(xr, yr):
        pos = lax.rem(px + xr, 4)
        return lax.div(pos, 2) * NC + lax.rem(y + yr, 4) * 4 + lax.rem(pos, 2) * 2 + core

    def x_dev(xr):
        return plane(slot(xr, 0))

    def y_dev(yr):
        return plane(slot(0, yr))

    partner_core = (z, c + 1 - 2 * core, h)
    partner_rep = (z, c, other)

    def send(src, dst, send_sem, recv_sem, device):
        pltpu.make_async_remote_copy(
            src_ref=src, dst_ref=dst, send_sem=send_sem, recv_sem=recv_sem,
            device_id=device, device_id_type=MESH,
        ).start()

    def arrived(ref, sem):
        pltpu.make_async_remote_copy(
            src_ref=ref, dst_ref=ref, send_sem=a_send, recv_sem=sem,
            device_id=partner_core, device_id_type=MESH,
        ).wait_recv()

    def sent(ref, sem):
        pltpu.make_async_remote_copy(
            src_ref=ref, dst_ref=ref, send_sem=sem, recv_sem=a_send,
            device_id=partner_core, device_id_type=MESH,
        ).wait_send()

    def columns(half):
        return pl.ds(pl.multiple_of(half * 256, 256), 256)

    loads = [
        pltpu.make_async_copy(src, dst, ld_sem.at[i])
        for i, (src, dst) in enumerate(
            [(od, od_v), (ou, ou_v), (master.at[:, columns(h)], master_v.at[:, columns(h)]),
             (tok, a_all.at[me]), (fd, fd_v), (og, og_v), (fu, fu_v), (md, old_moments.at[0]), (vd, old_moments.at[1]),
             (mu, old_moments.at[2]), (vu, old_moments.at[3]), (kd, flags.at[0]), (ku, flags.at[1]),
             (master.at[:, columns(other)], master_v.at[:, columns(other)])]
        )
    ]
    for load in loads:
        load.start()
    barrier = pltpu.get_barrier_semaphore()
    for d in (1, -1):
        pl.semaphore_signal(barrier, inc=1, device_id=ring(d), device_id_type=MESH)

    def greet_plane(d, carry):
        pl.semaphore_signal(barrier, inc=1, device_id=plane(lax.rem(me + d, 2 * NC)), device_id_type=MESH)
        return carry

    lax.fori_loop(1, 2 * NC, greet_plane, 0)

    for load in loads[:3]:
        load.wait()

    def merge(half):
        cols = columns(half)
        both = master_v[:, cols] + adapter_scale * split3(od_v[...], ou_v[:, cols])
        merged_v[:, cols] = both
        w_v[:, cols] = both.astype(BF16)
        return both.astype(BF16)

    b_all[z] = merge(h)
    pl.semaphore_wait(barrier, 2 * NC - 1 + 2)

    def tell(i, distance):
        for d in (distance, -distance):
            pl.semaphore_signal(far_sem.at[i], inc=1, device_id=ring(d), device_id_type=MESH)

    def told(i):
        pl.semaphore_wait(far_sem.at[i], 2)

    def chunk(zz, q):
        return b_all.at[zz, pl.ds((q % 2) * 256, 256), pl.ds((q // 2) * 128, 128)]

    def b_out(direction, step, q):
        sign = 1 if direction == 0 else -1
        origin = ring(-sign * (step - 1))[0]
        send(chunk(origin, q), chunk(origin, q), b_send, b_recv.at[direction, step - 1, q], ring(sign))

    def b_in(direction, step, q):
        sign = 1 if direction == 0 else -1
        origin = ring(-sign * step)[0]
        arrived(chunk(origin, q), b_recv.at[direction, step - 1, q])

    for q in range(4):
        for direction in (0, 1):
            b_out(direction, 1, q)

    tell(0, 1)

    for load in loads[3:7]:
        load.wait()
    down_cast = fd_v[...].astype(BF16)
    up_cast = fu_v[...].astype(BF16)
    hidden = jnp.dot(a_all[me], down_cast, preferred_element_type=F32)
    part[:, :, 0:128] = hidden.reshape(NC, 16, 128)
    backward = lax.dot_general(
        og_v[...], up_cast, (((1,), (1,)), ((), ())), preferred_element_type=F32
    )
    part[:, :, 128:256] = backward.reshape(NC, 16, 128)

    def rs_out(d, carry):
        to = lax.rem(c + d, NC)
        send(part.at[to], rs.at[d - 1], rs_send, rs_recv, (z, to, h))
        return carry

    lax.fori_loop(1, NC, rs_out, 0)

    forward = lax.select(core == 0, 3, 1)
    onward = lax.select(core == 0, 1, 3)

    def at(half, r1, r2):
        return a_all.at[slot(r1, r2) if half == 0 else slot(r2, r1), pl.ds(half * 128, 128)]

    def along(axis, r):
        return x_dev(r) if axis == 0 else y_dev(r)

    def a_out(ref, recv_sem, device):
        send(ref, ref, a_send, recv_sem, device)

    def core_out(half, r1, r2):
        a_out(at(half, r1, r2), c_recv.at[half, r1], partner_core)

    def p1_own(half):
        for d in (1, 3):
            a_out(at(half, 0, 0), p1_recv.at[half, 4 - d], along(half, d))

    def p2_own(half, r1):
        for d in (1, 3):
            a_out(at(half, r1, 0), p2_recv.at[half, r1, 4 - d], along(1 - half, d))
        core_out(half, r1, 0)

    def p1_near():
        for half in (0, 1):
            for r in (3, 1):
                arrived(at(half, r, 0), p1_recv.at[half, r])
            a_out(at(half, forward, 0), p1_recv.at[half, 2], along(half, onward))
        for half in (0, 1):
            p2_own(half, 3)
            p2_own(half, 1)

    def p1_far():
        for half in (0, 1):
            arrived(at(half, 2, 0), p1_recv.at[half, 2])
            p2_own(half, 2)

    def p2_near(half, r1):
        for r in (3, 1):
            arrived(at(half, r1, r), p2_recv.at[half, r1, r])
        a_out(at(half, r1, forward), p2_recv.at[half, r1, 2], along(1 - half, onward))
        core_out(half, r1, 3)
        core_out(half, r1, 1)

    def p2_far(half, r1):
        arrived(at(half, r1, 2), p2_recv.at[half, r1, 2])
        core_out(half, r1, 2)

    for half in (0, 1):
        p1_own(half)
    for half in (0, 1):
        p2_own(half, 0)

    loads[13].wait()
    merge(other)
    stores = [
        pltpu.make_async_copy(merged_v, merged, st_sem.at[2]),
        pltpu.make_async_copy(w_v, w, st_sem.at[3]),
    ]
    for store in stores:
        store.start()

    def sum_rows():
        arrived(rs, rs_recv)
        total = part[c]
        for d in range(NC - 1):
            total = total + rs[d]
        hb_all[me] = total.astype(BF16)

        def hb_out(d, carry):
            send(hb_all.at[me], hb_all.at[me], hb_send, hb_recv, plane(lax.rem(me + d, 2 * NC)))
            return carry

        lax.fori_loop(1, 2 * NC, hb_out, 0)

    def rows_of(hp):
        return hb_all[pl.ds(hp * NC, NC)].reshape(256, 256)

    def start_outputs():
        arrived(hb_all.at[pl.ds(0, 2 * NC - 1)], hb_recv)
        up_half = fu_v[:, columns(h)].astype(BF16)
        for hp in (0, 1):
            acc[hp] = adapter_scale * jnp.dot(rows_of(hp)[:, :128], up_half, preferred_element_type=F32)

    parity = lax.rem(z, 2)
    toward = lax.select(parity == core, 1, -1)

    def kept(u, gradient):
        gtmp[...] = (adapter_scale * gradient).reshape(NZ, 2, 16, 128)
        rows = gtmp[:, h].reshape(NZ // 2, 2, 16, 128)
        for p in (0, 1):
            gsum[p, :, u] = rows[:, p]

    def up_gradient():
        up = contract_rows(og_v[...], hb_all[pl.ds(h * NC, NC)].reshape(256, 256)[:, :128])
        kept(1, up)
        up_send[...] = gtmp[:, other].astype(BF16)
        send(up_send, up_recv, up_sem.at[0], up_sem.at[1], partner_rep)

    def gradients():
        down = jnp.zeros((512, 128), F32)
        for hp in (0, 1):
            down = down + contract_rows(a_all[hp * NC + c], rows_of(hp)[:, 128:])
        kept(0, down)
        arrived(up_recv, up_sem.at[1])
        rows = up_recv[...].astype(F32).reshape(NZ // 2, 2, 16, 128)
        for p in (0, 1):
            gsum[p, :, 1] += rows[:, p]
        pair_send[...] = gsum[1 - parity].astype(BF16)
        send(pair_send, pair_recv, pair_sem.at[0], pair_sem.at[1], ring(toward))

    def pair_gradients():
        arrived(pair_recv, pair_sem.at[1])
        gsum[parity] += pair_recv[...].astype(F32)
        gsend[...] = gsum[parity].astype(BF16)
        told(2)

        def g_out(d, carry):
            to = lax.rem(z + 2 * d, NZ)
            send(gsend.at[lax.div(to, 2)], grecv.at[d - 1], g_send, g_recv, (to, c, h))
            return carry

        lax.fori_loop(1, NZ // 2, g_out, 0)

    def sum_gradients():
        arrived(grecv, g_recv)
        for u in (0, 1):
            total = gsum[parity, lax.div(z, 2), u]
            for d in range(NZ // 2 - 1):
                total = total + grecv[d, u].astype(F32)
            gbuf[h, u] = total
        send(gbuf.at[h], gbuf.at[h], gx_sem.at[0], gx_sem.at[1], partner_rep)

    def end_gradients():
        arrived(gbuf.at[other], gx_sem.at[1])
        for load in loads[7:13]:
            load.wait()
        for u in (0, 1):
            for hp in (0, 1):
                rows = pl.ds(hp * 16, 16)
                keep = flags[u, hp].astype(F32)
                gradient = gbuf[hp, u]
                moments_v[2 * u, rows, :] = (beta_one * keep) * old_moments[2 * u, rows, :] + (1.0 - beta_one) * gradient
                moments_v[2 * u + 1, rows, :] = (beta_two * keep) * old_moments[2 * u + 1, rows, :] + (
                    (1.0 - beta_two) * gradient * gradient
                )
        store = pltpu.make_async_copy(moments_v, moments, st_sem.at[4])
        store.start()
        stores.append(store)

    def product(zz):
        def one(hp, carry):
            acc[hp] += jnp.dot(a_all[hp * NC + zz], b_all[zz], preferred_element_type=F32)
            return carry

        lax.fori_loop(0, 2, one, 0)

    def products(first, last):
        def one(s, carry):
            product(lax.rem(z + s, NZ))
            product(lax.rem(z + (NZ - s), NZ))
            return carry

        lax.fori_loop(first, last + 1, one, 0)

    def first_products():
        for half in (0, 1):
            for r1 in range(4):
                arrived(a_all.at[pl.ds(0, 2)], c_recv.at[half, r1])
        product(z)
        products(1, 1)

    def doubling():
        told(0)
        tell(1, 2)

    def doubled():
        told(1)
        tell(2, 4)

    after = {
        0: [doubling],
        2: [doubled],
        3: [sum_rows],
        4: [p1_near],
        6: [lambda: p2_near(1, 0), lambda: p2_near(0, 0)],
        7: [p1_far],
        10: [start_outputs, up_gradient],
        11: [lambda: p2_near(0, 3), lambda: p2_near(1, 3)],
        12: [lambda: p2_near(0, 1), lambda: p2_near(1, 1), lambda: p2_far(1, 0)],
        13: [lambda: p2_far(0, 0)],
        14: [gradients],
        15: [lambda: p2_near(0, 2), lambda: p2_near(1, 2)],
        18: [lambda: p2_far(0, 3), lambda: p2_far(1, 3)],
        19: [pair_gradients, lambda: p2_far(0, 1), lambda: p2_far(1, 1)],
        20: [lambda: p2_far(0, 2), lambda: p2_far(1, 2)],
        22: [first_products],
        23: [lambda: products(2, 3)],
        24: [lambda: products(4, 5)],
        25: [lambda: products(6, 6)],
        27: [lambda: products(7, 7), sum_gradients],
    }
    for tick in range(28):
        step, q = tick // 4 + 1, tick % 4
        for direction in (0, 1):
            b_in(direction, step, q)
            if step < 7 or q % 2 == direction:
                b_out(direction, step + 1, q)
        for action in after.get(tick, ()):
            action()

    far = lax.rem(z + 8, NZ)
    outs = []
    for part_of in (0, 1):
        for direction in (0, 1):
            b_in(direction, 8, 2 * part_of + direction)
        cols = pl.ds(part_of * 128, 128)
        there = pl.ds(pl.multiple_of(h * 256 + part_of * 128, 128), 128)
        for hp in (other, h):
            total = acc[hp, :, cols] + jnp.dot(
                a_all[hp * NC + far], b_all[far, :, cols], preferred_element_type=F32
            )
            stage[hp, part_of] = total.astype(BF16)
            if hp is other:
                send(stage.at[other, part_of], out.at[:, there], o_send.at[part_of], o_recv.at[part_of], partner_rep)
            else:
                keep = pltpu.make_async_copy(stage.at[h, part_of], out.at[:, there], st_sem.at[part_of])
                keep.start()
                stores.append(keep)

    end_gradients()
    for store in stores:
        store.wait()
    sent(a_all.at[pl.ds(0, 31)], a_send)
    sent(b_all.at[pl.ds(0, 15)], b_send)
    sent(rs, rs_send)
    sent(hb_all.at[pl.ds(0, 2 * NC - 1)], hb_send)
    sent(up_send, up_sem.at[0])
    sent(pair_send, pair_sem.at[0])
    sent(grecv, g_send)
    sent(gbuf.at[h], gx_sem.at[0])
    for part_of in (0, 1):
        sent(stage.at[other, part_of], o_send.at[part_of])
        there = pl.ds(pl.multiple_of(other * 256 + part_of * 128, 128), 128)
        arrived(out.at[:, there], o_recv.at[part_of])


def write_out(merged, w, out, moments, merged_to, w_to, out_to, md, vd, mu, vu, merged_v, w_v, out_v, moments_v, sem):
    loads, stores = [], []
    for src, mid, dst in ((merged, merged_v, merged_to), (w, w_v, w_to), (out, out_v, out_to)):
        half = src.shape[0] // 2
        for rows in (pl.ds(0, half), pl.ds(half, half)):
            loads.append(pltpu.make_async_copy(src.at[rows], mid.at[rows], sem.at[len(loads)]))
            stores.append([pltpu.make_async_copy(mid.at[rows], dst.at[rows], sem.at[7 + len(stores)])])
    loads.append(pltpu.make_async_copy(moments, moments_v, sem.at[6]))
    stores.append([pltpu.make_async_copy(moments_v.at[i], ref, sem.at[13 + i]) for i, ref in enumerate((md, vd, mu, vu))])
    for load in loads:
        load.start()
    for load, after in zip(loads, stores):
        load.wait()
        for store in after:
            store.start()
    for after in stores:
        for store in after:
            store.wait()


def body(
    tokens, output_gradient, master_weight, old_down, old_up, fresh_down, fresh_up,
    m_down, v_down, m_up, v_up, keep_down, keep_up,
):
    dma = pltpu.SemaphoreType.DMA
    vmem = pltpu.VMEM
    hbm = pl.BlockSpec(memory_space=pltpu.HBM)
    results = pl.pallas_call(
        kernel,
        out_shape=(
            jax.ShapeDtypeStruct((512, 512), F32),
            jax.ShapeDtypeStruct((512, 512), BF16),
            jax.ShapeDtypeStruct((256, 512), BF16),
            jax.ShapeDtypeStruct((4, 32, 128), F32),
        ),
        in_specs=[hbm] * 13,
        out_specs=(hbm,) * 4,
        scratch_shapes=[
            vmem((2 * NC, 256, 512), BF16),
            vmem((NZ, 512, 256), BF16),
            vmem((256, 512), BF16),
            vmem((512, 512), F32),
            vmem((512, 512), F32),
            vmem((512, 512), BF16),
            vmem((4, 32, 128), F32),
            vmem((512, 128), F32),
            vmem((128, 512), F32),
            vmem((512, 128), F32),
            vmem((128, 512), F32),
            vmem((NC, 16, 256), F32),
            vmem((NC - 1, 16, 256), F32),
            vmem((2 * NC, 16, 256), BF16),
            vmem((NZ, 2, 16, 128), F32),
            vmem((NZ, 16, 128), BF16),
            vmem((NZ, 16, 128), BF16),
            vmem((2, NZ // 2, 2, 16, 128), F32),
            vmem((NZ // 2, 2, 16, 128), BF16),
            vmem((NZ // 2, 2, 16, 128), BF16),
            vmem((NZ // 2, 2, 16, 128), BF16),
            vmem((NZ // 2 - 1, 2, 16, 128), BF16),
            vmem((2, 2, 16, 128), F32),
            vmem((2, 256, 256), F32),
            vmem((2, 2, 256, 128), BF16),
            vmem((4, 32, 128), F32),
            pltpu.SMEM((2, 2), jnp.int32),
            dma((14,)),
            dma((5,)),
            dma,
            dma((2, 8, 4)),
            dma((2, 4)),
            dma((2, 4, 4)),
            dma((2, 4)),
            dma,
            dma,
            dma,
            dma,
            dma,
            dma((2,)),
            dma((2,)),
            dma,
            dma,
            dma((2,)),
            dma((2,)),
            dma((2,)),
            pltpu.SemaphoreType.REGULAR((3,)),
        ],
        compiler_params=pltpu.CompilerParams(
            collective_id=0, has_side_effects=True, vmem_limit_bytes=60 * 1024 * 1024
        ),
        name="relora_step",
    )(
        tokens, output_gradient, master_weight, old_down, old_up, fresh_down, fresh_up,
        m_down, v_down, m_up.T, v_up.T, keep_down, keep_up,
    )
    small = jax.ShapeDtypeStruct((32, 128), F32)
    merged_weight, w_copy, outputs, md, vd, mu, vu = pl.pallas_call(
        write_out,
        out_shape=(
            jax.ShapeDtypeStruct((512, 512), F32),
            jax.ShapeDtypeStruct((512, 512), BF16),
            jax.ShapeDtypeStruct((256, 512), BF16),
            small, small, small, small,
        ),
        in_specs=[hbm] * 4,
        out_specs=(hbm,) * 7,
        scratch_shapes=[
            vmem((512, 512), F32), vmem((512, 512), BF16), vmem((256, 512), BF16), vmem((4, 32, 128), F32), dma((17,)),
        ],
        compiler_params=pltpu.CompilerParams(vmem_limit_bytes=60 * 1024 * 1024),
        name="write_out",
    )(*results)
    return (merged_weight, w_copy, outputs, md, vd, mu.T, vu.T)


def solution(mesh):
    both = P(("row", "rep"), "col")
    tile = P("row", "col")
    down = P(("col", "row"), None)
    up = P(None, ("col", "row"))
    flags = P(("col", "row"))
    return jax.shard_map(
        body,
        mesh=mesh,
        in_specs=(
            both, both, tile, P("row", None), P(None, "col"), P("col", None), P(None, "col"),
            down, down, up, up, flags, flags,
        ),
        out_specs=(tile, tile, both, down, down, up, up),
        check_vma=False,
    )
```

```python
import jax
import jax.numpy as jnp
from jax import lax
from jax.experimental import pallas as pl
from jax.experimental.pallas import tpu as pltpu
from jax.sharding import PartitionSpec as P

BLOCK = 16
adapter_scale = 0.25
beta_one = 0.9
beta_two = 0.95

MESH = pl.DeviceIdType.MESH
NZ = 16
NC = 16
F32 = jnp.float32
BF16 = jnp.bfloat16


def split3(lhs, rhs):
    lhs_hi = lhs.astype(BF16)
    lhs_lo = (lhs - lhs_hi.astype(F32)).astype(BF16)
    rhs_hi = rhs.astype(BF16)
    rhs_lo = (rhs - rhs_hi.astype(F32)).astype(BF16)
    dot = lambda a, b: jnp.dot(a, b, preferred_element_type=F32)
    return dot(lhs_hi, rhs_hi) + (dot(lhs_hi, rhs_lo) + dot(lhs_lo, rhs_hi))


def contract_rows(lhs, rhs):
    return lax.dot_general(lhs, rhs, (((0,), (0,)), ((), ())), preferred_element_type=F32)


def kernel(
    tok, og, master, od, ou, fd, fu, md, vd, mu, vu, kd, ku,
    merged, w, out, moments,
    a_all, b_all, og_v, master_v, merged_v, w_v, moments_v, od_v, ou_v, fd_v, fu_v,
    part, rs, hb_all, gtmp, up_send, up_recv, gsum, pair_send, pair_recv, gsend, grecv, gbuf, acc, stage, old_moments, flags,
    ld_sem, st_sem, b_send, b_recv, p1_recv, p2_recv, c_recv, a_send,
    rs_send, rs_recv, hb_send, hb_recv, up_sem, pair_sem, g_send, g_recv, gx_sem, o_send, o_recv, far_sem, b_last,
):
    z = lax.axis_index("row")
    c = lax.axis_index("col")
    h = lax.axis_index("rep")
    other = 1 - h
    y = lax.div(c, 4)
    lo = lax.rem(lax.div(c, 2), 2)
    core = lax.rem(c, 2)
    px = 2 * h + lo
    me = h * NC + c

    def ring(d):
        return (lax.rem(z + (d + NZ), NZ), c, h)

    def plane(j):
        return (z, lax.rem(j, NC), lax.div(j, NC))

    def slot(xr, yr):
        pos = lax.rem(px + xr, 4)
        return lax.div(pos, 2) * NC + lax.rem(y + yr, 4) * 4 + lax.rem(pos, 2) * 2 + core

    def x_dev(xr):
        return plane(slot(xr, 0))

    def y_dev(yr):
        return plane(slot(0, yr))

    partner_core = (z, c + 1 - 2 * core, h)
    partner_rep = (z, c, other)

    def send(src, dst, send_sem, recv_sem, device):
        pltpu.make_async_remote_copy(
            src_ref=src, dst_ref=dst, send_sem=send_sem, recv_sem=recv_sem,
            device_id=device, device_id_type=MESH,
        ).start()

    def arrived(ref, sem):
        pltpu.make_async_remote_copy(
            src_ref=ref, dst_ref=ref, send_sem=a_send, recv_sem=sem,
            device_id=partner_core, device_id_type=MESH,
        ).wait_recv()

    def sent(ref, sem):
        pltpu.make_async_remote_copy(
            src_ref=ref, dst_ref=ref, send_sem=sem, recv_sem=a_send,
            device_id=partner_core, device_id_type=MESH,
        ).wait_send()

    def columns(half):
        return pl.ds(pl.multiple_of(half * 256, 256), 256)

    loads = [
        pltpu.make_async_copy(src, dst, ld_sem.at[i])
        for i, (src, dst) in enumerate(
            [(od, od_v), (ou, ou_v), (master.at[:, columns(h)], master_v.at[:, columns(h)]),
             (tok, a_all.at[me]), (fd, fd_v), (og, og_v), (fu, fu_v), (md, old_moments.at[0]), (vd, old_moments.at[1]),
             (mu, old_moments.at[2]), (vu, old_moments.at[3]), (kd, flags.at[0]), (ku, flags.at[1]),
             (master.at[:, columns(other)], master_v.at[:, columns(other)])]
        )
    ]
    for load in loads:
        load.start()
    barrier = pltpu.get_barrier_semaphore()
    for d in (1, -1):
        pl.semaphore_signal(barrier, inc=1, device_id=ring(d), device_id_type=MESH)

    def greet_plane(d, carry):
        pl.semaphore_signal(barrier, inc=1, device_id=plane(lax.rem(me + d, 2 * NC)), device_id_type=MESH)
        return carry

    lax.fori_loop(1, 2 * NC, greet_plane, 0)

    for load in loads[:3]:
        load.wait()

    def merge(half):
        cols = columns(half)
        both = master_v[:, cols] + adapter_scale * split3(od_v[...], ou_v[:, cols])
        merged_v[:, cols] = both
        w_v[:, cols] = both.astype(BF16)
        return both.astype(BF16)

    b_all[z] = merge(h)
    pl.semaphore_wait(barrier, 2 * NC - 1 + 2)

    def tell(i, distance):
        for d in (distance, -distance):
            pl.semaphore_signal(far_sem.at[i], inc=1, device_id=ring(d), device_id_type=MESH)

    def told(i):
        pl.semaphore_wait(far_sem.at[i], 2)

    def chunk(zz, q):
        return b_all.at[zz, pl.ds((q % 2) * 256, 256), pl.ds((q // 2) * 128, 128)]

    def b_out(direction, step, q, send_sem=b_send):
        sign = 1 if direction == 0 else -1
        origin = ring(-sign * (step - 1))[0]
        send(chunk(origin, q), chunk(origin, q), send_sem, b_recv.at[direction, step - 1, q], ring(sign))

    def b_in(direction, step, q):
        sign = 1 if direction == 0 else -1
        origin = ring(-sign * step)[0]
        arrived(chunk(origin, q), b_recv.at[direction, step - 1, q])

    for q in range(4):
        for direction in (0, 1):
            b_out(direction, 1, q)

    tell(0, 1)

    for load in loads[3:7]:
        load.wait()
    down_cast = fd_v[...].astype(BF16)
    up_cast = fu_v[...].astype(BF16)
    hidden = jnp.dot(a_all[me], down_cast, preferred_element_type=F32)
    part[:, :, 0:128] = hidden.reshape(NC, 16, 128)
    backward = lax.dot_general(
        og_v[...], up_cast, (((1,), (1,)), ((), ())), preferred_element_type=F32
    )
    part[:, :, 128:256] = backward.reshape(NC, 16, 128)

    def rs_out(d, carry):
        to = lax.rem(c + d, NC)
        send(part.at[to], rs.at[d - 1], rs_send, rs_recv, (z, to, h))
        return carry

    lax.fori_loop(1, NC, rs_out, 0)

    forward = lax.select(core == 0, 3, 1)
    onward = lax.select(core == 0, 1, 3)

    def at(half, r1, r2):
        return a_all.at[slot(r1, r2) if half == 0 else slot(r2, r1), pl.ds(half * 128, 128)]

    def along(axis, r):
        return x_dev(r) if axis == 0 else y_dev(r)

    def a_out(ref, recv_sem, device):
        send(ref, ref, a_send, recv_sem, device)

    def core_out(half, r1, r2):
        a_out(at(half, r1, r2), c_recv.at[half, r1], partner_core)

    def p1_own(half):
        for d in (1, 3):
            a_out(at(half, 0, 0), p1_recv.at[half, 4 - d], along(half, d))

    def p2_own(half, r1):
        for d in (1, 3):
            a_out(at(half, r1, 0), p2_recv.at[half, r1, 4 - d], along(1 - half, d))
        core_out(half, r1, 0)

    def p1_near():
        for half in (0, 1):
            for r in (3, 1):
                arrived(at(half, r, 0), p1_recv.at[half, r])
            a_out(at(half, forward, 0), p1_recv.at[half, 2], along(half, onward))
        for half in (0, 1):
            p2_own(half, 3)
            p2_own(half, 1)

    def p1_far():
        for half in (0, 1):
            arrived(at(half, 2, 0), p1_recv.at[half, 2])
            p2_own(half, 2)

    def p2_near(half, r1):
        for r in (3, 1):
            arrived(at(half, r1, r), p2_recv.at[half, r1, r])
        a_out(at(half, r1, forward), p2_recv.at[half, r1, 2], along(1 - half, onward))
        core_out(half, r1, 3)
        core_out(half, r1, 1)

    def p2_far(half, r1):
        arrived(at(half, r1, 2), p2_recv.at[half, r1, 2])
        core_out(half, r1, 2)

    for half in (0, 1):
        p1_own(half)
    for half in (0, 1):
        p2_own(half, 0)

    loads[13].wait()
    merge(other)
    stores = [
        pltpu.make_async_copy(merged_v, merged, st_sem.at[2]),
        pltpu.make_async_copy(w_v, w, st_sem.at[3]),
    ]
    for store in stores:
        store.start()

    def sum_rows():
        arrived(rs, rs_recv)
        total = part[c]
        for d in range(NC - 1):
            total = total + rs[d]
        hb_all[me] = total.astype(BF16)

        def hb_out(d, carry):
            send(hb_all.at[me], hb_all.at[me], hb_send, hb_recv, plane(lax.rem(me + d, 2 * NC)))
            return carry

        lax.fori_loop(1, 2 * NC, hb_out, 0)

    def rows_of(hp):
        return hb_all[pl.ds(hp * NC, NC)].reshape(256, 256)

    def start_outputs():
        arrived(hb_all.at[pl.ds(0, 2 * NC - 1)], hb_recv)
        up_half = fu_v[:, columns(h)].astype(BF16)
        for hp in (0, 1):
            acc[hp] = adapter_scale * jnp.dot(rows_of(hp)[:, :128], up_half, preferred_element_type=F32)

    parity = lax.rem(z, 2)
    toward = lax.select(parity == core, 1, -1)

    def kept(u, gradient):
        gtmp[...] = (adapter_scale * gradient).reshape(NZ, 2, 16, 128)
        rows = gtmp[:, h].reshape(NZ // 2, 2, 16, 128)
        for p in (0, 1):
            gsum[p, :, u] = rows[:, p]

    def up_gradient():
        up = contract_rows(og_v[...], hb_all[pl.ds(h * NC, NC)].reshape(256, 256)[:, :128])
        kept(1, up)
        up_send[...] = gtmp[:, other].astype(BF16)
        send(up_send, up_recv, up_sem.at[0], up_sem.at[1], partner_rep)

    def gradients():
        down = jnp.zeros((512, 128), F32)
        for hp in (0, 1):
            down = down + contract_rows(a_all[hp * NC + c], rows_of(hp)[:, 128:])
        kept(0, down)
        arrived(up_recv, up_sem.at[1])
        rows = up_recv[...].astype(F32).reshape(NZ // 2, 2, 16, 128)
        for p in (0, 1):
            gsum[p, :, 1] += rows[:, p]
        pair_send[...] = gsum[1 - parity].astype(BF16)
        send(pair_send, pair_recv, pair_sem.at[0], pair_sem.at[1], ring(toward))

    def pair_gradients():
        arrived(pair_recv, pair_sem.at[1])
        gsum[parity] += pair_recv[...].astype(F32)
        gsend[...] = gsum[parity].astype(BF16)
        told(2)

        def g_out(d, carry):
            to = lax.rem(z + 2 * d, NZ)
            send(gsend.at[lax.div(to, 2)], grecv.at[d - 1], g_send, g_recv, (to, c, h))
            return carry

        lax.fori_loop(1, NZ // 2, g_out, 0)

    def sum_gradients():
        arrived(grecv, g_recv)
        for u in (0, 1):
            total = gsum[parity, lax.div(z, 2), u]
            for d in range(NZ // 2 - 1):
                total = total + grecv[d, u].astype(F32)
            gbuf[h, u] = total
        send(gbuf.at[h], gbuf.at[h], gx_sem.at[0], gx_sem.at[1], partner_rep)

    def end_gradients():
        arrived(gbuf.at[other], gx_sem.at[1])
        for load in loads[7:13]:
            load.wait()
        for u in (0, 1):
            for hp in (0, 1):
                rows = pl.ds(hp * 16, 16)
                keep = flags[u, hp].astype(F32)
                gradient = gbuf[hp, u]
                moments_v[2 * u, rows, :] = (beta_one * keep) * old_moments[2 * u, rows, :] + (1.0 - beta_one) * gradient
                moments_v[2 * u + 1, rows, :] = (beta_two * keep) * old_moments[2 * u + 1, rows, :] + (
                    (1.0 - beta_two) * gradient * gradient
                )
        store = pltpu.make_async_copy(moments_v, moments, st_sem.at[4])
        store.start()
        stores.append(store)

    def product(zz):
        def one(hp, carry):
            acc[hp] += jnp.dot(a_all[hp * NC + zz], b_all[zz], preferred_element_type=F32)
            return carry

        lax.fori_loop(0, 2, one, 0)

    def products(first, last):
        def one(s, carry):
            product(lax.rem(z + s, NZ))
            product(lax.rem(z + (NZ - s), NZ))
            return carry

        lax.fori_loop(first, last + 1, one, 0)

    def first_products():
        for half in (0, 1):
            for r1 in range(4):
                arrived(a_all.at[pl.ds(0, 2)], c_recv.at[half, r1])
        product(z)
        products(1, 1)

    def doubling():
        told(0)
        tell(1, 2)

    def doubled():
        told(1)
        tell(2, 4)

    after = {
        0: [doubling],
        2: [doubled],
        3: [sum_rows],
        4: [p1_near],
        6: [lambda: p2_near(1, 0), lambda: p2_near(0, 0)],
        7: [p1_far],
        10: [start_outputs, up_gradient],
        11: [lambda: p2_near(0, 3), lambda: p2_near(1, 3)],
        12: [lambda: p2_near(0, 1), lambda: p2_near(1, 1), lambda: p2_far(1, 0)],
        13: [lambda: p2_far(0, 0)],
        14: [gradients],
        15: [lambda: p2_near(0, 2), lambda: p2_near(1, 2)],
        18: [lambda: p2_far(0, 3), lambda: p2_far(1, 3)],
        19: [pair_gradients, lambda: p2_far(0, 1), lambda: p2_far(1, 1)],
        20: [lambda: p2_far(0, 2), lambda: p2_far(1, 2)],
        22: [first_products],
        23: [lambda: products(2, 3)],
        24: [lambda: products(4, 5)],
        25: [lambda: products(6, 6)],
        27: [lambda: products(7, 7), sum_gradients],
    }
    for tick in range(28):
        step, q = tick // 4 + 1, tick % 4
        for direction in (0, 1):
            b_in(direction, step, q)
            if step < 7:
                b_out(direction, step + 1, q)
            elif q % 2 == 1 and direction == 1:
                b_out(1, 8, q, b_last.at[0])
            elif q % 2 == 0 and direction == 0:
                pl.when(z < NZ - 1)(lambda q=q: b_out(0, 8, q, b_last.at[1]))
            elif q % 2 == 0 and direction == 1:
                pl.when(z == 1)(lambda q=q: b_out(1, 8, q, b_last.at[2]))
        for action in after.get(tick, ()):
            action()

    far = lax.rem(z + 8, NZ)
    outs = []
    for part_of in (0, 1):
        pl.when(z > 0)(lambda q=2 * part_of: b_in(0, 8, q))
        pl.when(z == 0)(lambda q=2 * part_of: b_in(1, 8, q))
        b_in(1, 8, 2 * part_of + 1)
        cols = pl.ds(part_of * 128, 128)
        there = pl.ds(pl.multiple_of(h * 256 + part_of * 128, 128), 128)
        for hp in (other, h):
            total = acc[hp, :, cols] + jnp.dot(
                a_all[hp * NC + far], b_all[far, :, cols], preferred_element_type=F32
            )
            stage[hp, part_of] = total.astype(BF16)
            if hp is other:
                send(stage.at[other, part_of], out.at[:, there], o_send.at[part_of], o_recv.at[part_of], partner_rep)
            else:
                keep = pltpu.make_async_copy(stage.at[h, part_of], out.at[:, there], st_sem.at[part_of])
                keep.start()
                stores.append(keep)

    end_gradients()
    for store in stores:
        store.wait()
    sent(a_all.at[pl.ds(0, 31)], a_send)
    sent(b_all.at[pl.ds(0, 14)], b_send)
    two = b_all.at[0, pl.ds(0, 256)]
    sent(two, b_last.at[0])
    pl.when(z < NZ - 1)(lambda: sent(two, b_last.at[1]))
    pl.when(z == 1)(lambda: sent(two, b_last.at[2]))
    sent(rs, rs_send)
    sent(hb_all.at[pl.ds(0, 2 * NC - 1)], hb_send)
    sent(up_send, up_sem.at[0])
    sent(pair_send, pair_sem.at[0])
    sent(grecv, g_send)
    sent(gbuf.at[h], gx_sem.at[0])
    for part_of in (0, 1):
        sent(stage.at[other, part_of], o_send.at[part_of])
        there = pl.ds(pl.multiple_of(other * 256 + part_of * 128, 128), 128)
        arrived(out.at[:, there], o_recv.at[part_of])


def write_out(merged, w, out, moments, merged_to, w_to, out_to, md, vd, mu, vu, merged_v, w_v, out_v, moments_v, sem):
    loads, stores = [], []
    for src, mid, dst in ((merged, merged_v, merged_to), (w, w_v, w_to), (out, out_v, out_to)):
        half = src.shape[0] // 2
        for rows in (pl.ds(0, half), pl.ds(half, half)):
            loads.append(pltpu.make_async_copy(src.at[rows], mid.at[rows], sem.at[len(loads)]))
            stores.append([pltpu.make_async_copy(mid.at[rows], dst.at[rows], sem.at[7 + len(stores)])])
    loads.append(pltpu.make_async_copy(moments, moments_v, sem.at[6]))
    stores.append([pltpu.make_async_copy(moments_v.at[i], ref, sem.at[13 + i]) for i, ref in enumerate((md, vd, mu, vu))])
    for load in loads:
        load.start()
    for load, after in zip(loads, stores):
        load.wait()
        for store in after:
            store.start()
    for after in stores:
        for store in after:
            store.wait()


def body(
    tokens, output_gradient, master_weight, old_down, old_up, fresh_down, fresh_up,
    m_down, v_down, m_up, v_up, keep_down, keep_up,
):
    dma = pltpu.SemaphoreType.DMA
    vmem = pltpu.VMEM
    hbm = pl.BlockSpec(memory_space=pltpu.HBM)
    results = pl.pallas_call(
        kernel,
        out_shape=(
            jax.ShapeDtypeStruct((512, 512), F32),
            jax.ShapeDtypeStruct((512, 512), BF16),
            jax.ShapeDtypeStruct((256, 512), BF16),
            jax.ShapeDtypeStruct((4, 32, 128), F32),
        ),
        in_specs=[hbm] * 13,
        out_specs=(hbm,) * 4,
        scratch_shapes=[
            vmem((2 * NC, 256, 512), BF16),
            vmem((NZ, 512, 256), BF16),
            vmem((256, 512), BF16),
            vmem((512, 512), F32),
            vmem((512, 512), F32),
            vmem((512, 512), BF16),
            vmem((4, 32, 128), F32),
            vmem((512, 128), F32),
            vmem((128, 512), F32),
            vmem((512, 128), F32),
            vmem((128, 512), F32),
            vmem((NC, 16, 256), F32),
            vmem((NC - 1, 16, 256), F32),
            vmem((2 * NC, 16, 256), BF16),
            vmem((NZ, 2, 16, 128), F32),
            vmem((NZ, 16, 128), BF16),
            vmem((NZ, 16, 128), BF16),
            vmem((2, NZ // 2, 2, 16, 128), F32),
            vmem((NZ // 2, 2, 16, 128), BF16),
            vmem((NZ // 2, 2, 16, 128), BF16),
            vmem((NZ // 2, 2, 16, 128), BF16),
            vmem((NZ // 2 - 1, 2, 16, 128), BF16),
            vmem((2, 2, 16, 128), F32),
            vmem((2, 256, 256), F32),
            vmem((2, 2, 256, 128), BF16),
            vmem((4, 32, 128), F32),
            pltpu.SMEM((2, 2), jnp.int32),
            dma((14,)),
            dma((5,)),
            dma,
            dma((2, 8, 4)),
            dma((2, 4)),
            dma((2, 4, 4)),
            dma((2, 4)),
            dma,
            dma,
            dma,
            dma,
            dma,
            dma((2,)),
            dma((2,)),
            dma,
            dma,
            dma((2,)),
            dma((2,)),
            dma((2,)),
            pltpu.SemaphoreType.REGULAR((3,)),
            dma((3,)),
        ],
        compiler_params=pltpu.CompilerParams(
            collective_id=0, has_side_effects=True, vmem_limit_bytes=60 * 1024 * 1024
        ),
        name="relora_step",
    )(
        tokens, output_gradient, master_weight, old_down, old_up, fresh_down, fresh_up,
        m_down, v_down, m_up.T, v_up.T, keep_down, keep_up,
    )
    small = jax.ShapeDtypeStruct((32, 128), F32)
    merged_weight, w_copy, outputs, md, vd, mu, vu = pl.pallas_call(
        write_out,
        out_shape=(
            jax.ShapeDtypeStruct((512, 512), F32),
            jax.ShapeDtypeStruct((512, 512), BF16),
            jax.ShapeDtypeStruct((256, 512), BF16),
            small, small, small, small,
        ),
        in_specs=[hbm] * 4,
        out_specs=(hbm,) * 7,
        scratch_shapes=[
            vmem((512, 512), F32), vmem((512, 512), BF16), vmem((256, 512), BF16), vmem((4, 32, 128), F32), dma((17,)),
        ],
        compiler_params=pltpu.CompilerParams(vmem_limit_bytes=60 * 1024 * 1024),
        name="write_out",
    )(*results)
    return (merged_weight, w_copy, outputs, md, vd, mu.T, vu.T)


def solution(mesh):
    both = P(("row", "rep"), "col")
    tile = P("row", "col")
    down = P(("col", "row"), None)
    up = P(None, ("col", "row"))
    flags = P(("col", "row"))
    return jax.shard_map(
        body,
        mesh=mesh,
        in_specs=(
            both, both, tile, P("row", None), P(None, "col"), P("col", None), P(None, "col"),
            down, down, up, up, flags, flags,
        ),
        out_specs=(tile, tile, both, down, down, up, up),
        check_vma=False,
    )
```

```python
import jax
import jax.numpy as jnp
from jax import lax
from jax.experimental import pallas as pl
from jax.experimental.pallas import tpu as pltpu
from jax.sharding import PartitionSpec as P

BLOCK = 16
adapter_scale = 0.25
beta_one = 0.9
beta_two = 0.95

MESH = pl.DeviceIdType.MESH
NZ = 16
NC = 16
F32 = jnp.float32
BF16 = jnp.bfloat16


def split3(lhs, rhs):
    lhs_hi = lhs.astype(BF16)
    lhs_lo = (lhs - lhs_hi.astype(F32)).astype(BF16)
    rhs_hi = rhs.astype(BF16)
    rhs_lo = (rhs - rhs_hi.astype(F32)).astype(BF16)
    dot = lambda a, b: jnp.dot(a, b, preferred_element_type=F32)
    return dot(lhs_hi, rhs_hi) + (dot(lhs_hi, rhs_lo) + dot(lhs_lo, rhs_hi))


def contract_rows(lhs, rhs):
    return lax.dot_general(lhs, rhs, (((0,), (0,)), ((), ())), preferred_element_type=F32)


def kernel(
    tok, og, master, od, ou, fd, fu, md, vd, mu, vu, kd, ku,
    merged, w, out, moments,
    a_all, b_all, og_v, master_v, merged_v, w_v, moments_v, od_v, ou_v, fd_v, fu_v,
    part, rs, hb_all, gtmp, up_send, up_recv, gsum, pair_send, pair_recv, gsend, grecv, gbuf, acc, stage, old_moments, flags,
    ld_sem, st_sem, b_send, b_recv, p1_recv, p2_recv, c_recv, a_send,
    rs_send, rs_recv, hb_send, hb_recv, up_sem, pair_sem, g_send, g_recv, gx_sem, o_send, o_recv, far_sem, b_last,
):
    z = lax.axis_index("row")
    c = lax.axis_index("col")
    h = lax.axis_index("rep")
    other = 1 - h
    y = lax.div(c, 4)
    lo = lax.rem(lax.div(c, 2), 2)
    core = lax.rem(c, 2)
    px = 2 * h + lo
    me = h * NC + c

    def ring(d):
        return (lax.rem(z + (d + NZ), NZ), c, h)

    def plane(j):
        return (z, lax.rem(j, NC), lax.div(j, NC))

    def slot(xr, yr):
        pos = lax.rem(px + xr, 4)
        return lax.div(pos, 2) * NC + lax.rem(y + yr, 4) * 4 + lax.rem(pos, 2) * 2 + core

    def x_dev(xr):
        return plane(slot(xr, 0))

    def y_dev(yr):
        return plane(slot(0, yr))

    partner_core = (z, c + 1 - 2 * core, h)
    partner_rep = (z, c, other)

    def send(src, dst, send_sem, recv_sem, device):
        pltpu.make_async_remote_copy(
            src_ref=src, dst_ref=dst, send_sem=send_sem, recv_sem=recv_sem,
            device_id=device, device_id_type=MESH,
        ).start()

    def arrived(ref, sem):
        pltpu.make_async_remote_copy(
            src_ref=ref, dst_ref=ref, send_sem=a_send, recv_sem=sem,
            device_id=partner_core, device_id_type=MESH,
        ).wait_recv()

    def sent(ref, sem):
        pltpu.make_async_remote_copy(
            src_ref=ref, dst_ref=ref, send_sem=sem, recv_sem=a_send,
            device_id=partner_core, device_id_type=MESH,
        ).wait_send()

    def columns(half):
        return pl.ds(pl.multiple_of(half * 256, 256), 256)

    loads = [
        pltpu.make_async_copy(src, dst, ld_sem.at[i])
        for i, (src, dst) in enumerate(
            [(od, od_v), (ou, ou_v), (master.at[:, columns(h)], master_v.at[:, columns(h)]),
             (tok, a_all.at[me]), (fd, fd_v), (og, og_v), (fu, fu_v), (md, old_moments.at[0]), (vd, old_moments.at[1]),
             (mu, old_moments.at[2]), (vu, old_moments.at[3]), (kd, flags.at[0]), (ku, flags.at[1]),
             (master.at[:, columns(other)], master_v.at[:, columns(other)])]
        )
    ]
    for load in loads[:3]:
        load.start()
    barrier = pltpu.get_barrier_semaphore()
    for d in (1, -1):
        pl.semaphore_signal(barrier, inc=1, device_id=ring(d), device_id_type=MESH)

    def greet_plane(d, carry):
        pl.semaphore_signal(barrier, inc=1, device_id=plane(lax.rem(me + d, 2 * NC)), device_id_type=MESH)
        return carry

    lax.fori_loop(1, 2 * NC, greet_plane, 0)
    for load in loads[3:]:
        load.start()

    for load in loads[:3]:
        load.wait()

    def merge(first, length):
        cols = pl.ds(pl.multiple_of(first, 128), length)
        both = master_v[:, cols] + adapter_scale * split3(od_v[...], ou_v[:, cols])
        merged_v[:, cols] = both
        w_v[:, cols] = both.astype(BF16)
        return both.astype(BF16)

    b_all[z, :, 0:128] = merge(h * 256, 128)
    pl.semaphore_wait(barrier, 2 * NC - 1 + 2)

    def tell(i, distance):
        for d in (distance, -distance):
            pl.semaphore_signal(far_sem.at[i], inc=1, device_id=ring(d), device_id_type=MESH)

    def told(i):
        pl.semaphore_wait(far_sem.at[i], 2)

    def chunk(zz, q):
        return b_all.at[zz, pl.ds((q % 2) * 256, 256), pl.ds((q // 2) * 128, 128)]

    def b_out(direction, step, q, send_sem=b_send):
        sign = 1 if direction == 0 else -1
        origin = ring(-sign * (step - 1))[0]
        send(chunk(origin, q), chunk(origin, q), send_sem, b_recv.at[direction, step - 1, q], ring(sign))

    def b_in(direction, step, q):
        sign = 1 if direction == 0 else -1
        origin = ring(-sign * step)[0]
        arrived(chunk(origin, q), b_recv.at[direction, step - 1, q])

    for q in range(4):
        if q == 2:
            b_all[z, :, 128:256] = merge(h * 256 + 128, 128)
        for direction in (0, 1):
            b_out(direction, 1, q)

    tell(0, 1)

    for load in loads[3:7]:
        load.wait()
    down_cast = fd_v[...].astype(BF16)
    up_cast = fu_v[...].astype(BF16)
    hidden = jnp.dot(a_all[me], down_cast, preferred_element_type=F32)
    part[:, :, 0:128] = hidden.reshape(NC, 16, 128)
    backward = lax.dot_general(
        og_v[...], up_cast, (((1,), (1,)), ((), ())), preferred_element_type=F32
    )
    part[:, :, 128:256] = backward.reshape(NC, 16, 128)

    def rs_out(d, carry):
        to = lax.rem(c + d, NC)
        send(part.at[to], rs.at[d - 1], rs_send, rs_recv, (z, to, h))
        return carry

    lax.fori_loop(1, NC, rs_out, 0)

    forward = lax.select(core == 0, 3, 1)
    onward = lax.select(core == 0, 1, 3)

    def at(half, r1, r2):
        return a_all.at[slot(r1, r2) if half == 0 else slot(r2, r1), pl.ds(half * 128, 128)]

    def along(axis, r):
        return x_dev(r) if axis == 0 else y_dev(r)

    def a_out(ref, recv_sem, device):
        send(ref, ref, a_send, recv_sem, device)

    def core_out(half, r1, r2):
        a_out(at(half, r1, r2), c_recv.at[half, r1], partner_core)

    def p1_own(half):
        for d in (1, 3):
            a_out(at(half, 0, 0), p1_recv.at[half, 4 - d], along(half, d))

    def p2_own(half, r1):
        for d in (1, 3):
            a_out(at(half, r1, 0), p2_recv.at[half, r1, 4 - d], along(1 - half, d))
        core_out(half, r1, 0)

    def p1_near():
        for half in (0, 1):
            for r in (3, 1):
                arrived(at(half, r, 0), p1_recv.at[half, r])
            a_out(at(half, forward, 0), p1_recv.at[half, 2], along(half, onward))
        for half in (0, 1):
            p2_own(half, 3)
            p2_own(half, 1)

    def p1_far():
        for half in (0, 1):
            arrived(at(half, 2, 0), p1_recv.at[half, 2])
            p2_own(half, 2)

    def p2_near(half, r1):
        for r in (3, 1):
            arrived(at(half, r1, r), p2_recv.at[half, r1, r])
        a_out(at(half, r1, forward), p2_recv.at[half, r1, 2], along(1 - half, onward))
        core_out(half, r1, 3)
        core_out(half, r1, 1)

    def p2_far(half, r1):
        arrived(at(half, r1, 2), p2_recv.at[half, r1, 2])
        core_out(half, r1, 2)

    for half in (0, 1):
        p1_own(half)
    for half in (0, 1):
        p2_own(half, 0)

    loads[13].wait()
    merge(other * 256, 256)
    stores = [
        pltpu.make_async_copy(merged_v, merged, st_sem.at[2]),
        pltpu.make_async_copy(w_v, w, st_sem.at[3]),
    ]
    for store in stores:
        store.start()

    def sum_rows():
        arrived(rs, rs_recv)
        total = part[c]
        for d in range(NC - 1):
            total = total + rs[d]
        hb_all[me] = total.astype(BF16)

        def hb_out(d, carry):
            send(hb_all.at[me], hb_all.at[me], hb_send, hb_recv, plane(lax.rem(me + d, 2 * NC)))
            return carry

        lax.fori_loop(1, 2 * NC, hb_out, 0)

    def rows_of(hp):
        return hb_all[pl.ds(hp * NC, NC)].reshape(256, 256)

    def start_outputs():
        arrived(hb_all.at[pl.ds(0, 2 * NC - 1)], hb_recv)
        up_half = fu_v[:, columns(h)].astype(BF16)
        for hp in (0, 1):
            acc[hp] = adapter_scale * jnp.dot(rows_of(hp)[:, :128], up_half, preferred_element_type=F32)

    parity = lax.rem(z, 2)
    toward = lax.select(parity == core, 1, -1)

    def kept(u, gradient):
        gtmp[...] = (adapter_scale * gradient).reshape(NZ, 2, 16, 128)
        rows = gtmp[:, h].reshape(NZ // 2, 2, 16, 128)
        for p in (0, 1):
            gsum[p, :, u] = rows[:, p]

    def up_gradient():
        up = contract_rows(og_v[...], hb_all[pl.ds(h * NC, NC)].reshape(256, 256)[:, :128])
        kept(1, up)
        up_send[...] = gtmp[:, other].astype(BF16)
        send(up_send, up_recv, up_sem.at[0], up_sem.at[1], partner_rep)

    def gradients():
        down = jnp.zeros((512, 128), F32)
        for hp in (0, 1):
            down = down + contract_rows(a_all[hp * NC + c], rows_of(hp)[:, 128:])
        kept(0, down)
        arrived(up_recv, up_sem.at[1])
        rows = up_recv[...].astype(F32).reshape(NZ // 2, 2, 16, 128)
        for p in (0, 1):
            gsum[p, :, 1] += rows[:, p]
        pair_send[...] = gsum[1 - parity].astype(BF16)
        send(pair_send, pair_recv, pair_sem.at[0], pair_sem.at[1], ring(toward))

    def pair_gradients():
        arrived(pair_recv, pair_sem.at[1])
        gsum[parity] += pair_recv[...].astype(F32)
        gsend[...] = gsum[parity].astype(BF16)
        told(2)

        def g_out(d, carry):
            to = lax.rem(z + 2 * d, NZ)
            send(gsend.at[lax.div(to, 2)], grecv.at[d - 1], g_send, g_recv, (to, c, h))
            return carry

        lax.fori_loop(1, NZ // 2, g_out, 0)

    def sum_gradients():
        arrived(grecv, g_recv)
        for u in (0, 1):
            total = gsum[parity, lax.div(z, 2), u]
            for d in range(NZ // 2 - 1):
                total = total + grecv[d, u].astype(F32)
            gbuf[h, u] = total
        send(gbuf.at[h], gbuf.at[h], gx_sem.at[0], gx_sem.at[1], partner_rep)

    def end_gradients():
        arrived(gbuf.at[other], gx_sem.at[1])
        for load in loads[7:13]:
            load.wait()
        for u in (0, 1):
            for hp in (0, 1):
                rows = pl.ds(hp * 16, 16)
                keep = flags[u, hp].astype(F32)
                gradient = gbuf[hp, u]
                moments_v[2 * u, rows, :] = (beta_one * keep) * old_moments[2 * u, rows, :] + (1.0 - beta_one) * gradient
                moments_v[2 * u + 1, rows, :] = (beta_two * keep) * old_moments[2 * u + 1, rows, :] + (
                    (1.0 - beta_two) * gradient * gradient
                )
        store = pltpu.make_async_copy(moments_v, moments, st_sem.at[4])
        store.start()
        stores.append(store)

    def product(zz):
        def one(hp, carry):
            acc[hp] += jnp.dot(a_all[hp * NC + zz], b_all[zz], preferred_element_type=F32)
            return carry

        lax.fori_loop(0, 2, one, 0)

    def products(first, last):
        def one(s, carry):
            product(lax.rem(z + s, NZ))
            product(lax.rem(z + (NZ - s), NZ))
            return carry

        lax.fori_loop(first, last + 1, one, 0)

    def first_products():
        for half in (0, 1):
            for r1 in range(4):
                arrived(a_all.at[pl.ds(0, 2)], c_recv.at[half, r1])
        product(z)
        products(1, 1)

    def doubling():
        told(0)
        tell(1, 2)

    def doubled():
        told(1)
        tell(2, 4)

    after = {
        0: [doubling],
        2: [doubled],
        3: [sum_rows],
        4: [p1_near],
        6: [lambda: p2_near(1, 0), lambda: p2_near(0, 0)],
        7: [p1_far],
        10: [start_outputs, up_gradient],
        11: [lambda: p2_near(0, 3), lambda: p2_near(1, 3)],
        12: [lambda: p2_near(0, 1), lambda: p2_near(1, 1), lambda: p2_far(1, 0)],
        13: [lambda: p2_far(0, 0)],
        14: [gradients],
        15: [lambda: p2_near(0, 2), lambda: p2_near(1, 2)],
        18: [lambda: p2_far(0, 3), lambda: p2_far(1, 3)],
        19: [pair_gradients, lambda: p2_far(0, 1), lambda: p2_far(1, 1)],
        20: [lambda: p2_far(0, 2), lambda: p2_far(1, 2)],
        22: [first_products],
        23: [lambda: products(2, 3)],
        24: [lambda: products(4, 5)],
        25: [lambda: products(6, 6)],
        27: [lambda: products(7, 7), sum_gradients],
    }
    for tick in range(28):
        step, q = tick // 4 + 1, tick % 4
        for direction in (0, 1):
            b_in(direction, step, q)
            if step < 7:
                b_out(direction, step + 1, q)
            elif q % 2 == 1 and direction == 1:
                b_out(1, 8, q, b_last.at[0])
            elif q % 2 == 0 and direction == 0:
                pl.when(z < NZ - 1)(lambda q=q: b_out(0, 8, q, b_last.at[1]))
            elif q % 2 == 0 and direction == 1:
                pl.when(z == 1)(lambda q=q: b_out(1, 8, q, b_last.at[2]))
        for action in after.get(tick, ()):
            action()

    far = lax.rem(z + 8, NZ)
    outs = []
    for part_of in (0, 1):
        pl.when(z > 0)(lambda q=2 * part_of: b_in(0, 8, q))
        pl.when(z == 0)(lambda q=2 * part_of: b_in(1, 8, q))
        b_in(1, 8, 2 * part_of + 1)
        cols = pl.ds(part_of * 128, 128)
        there = pl.ds(pl.multiple_of(h * 256 + part_of * 128, 128), 128)
        for hp in (other, h):
            total = acc[hp, :, cols] + jnp.dot(
                a_all[hp * NC + far], b_all[far, :, cols], preferred_element_type=F32
            )
            stage[hp, part_of] = total.astype(BF16)
            if hp is other:
                send(stage.at[other, part_of], out.at[:, there], o_send.at[part_of], o_recv.at[part_of], partner_rep)
            else:
                keep = pltpu.make_async_copy(stage.at[h, part_of], out.at[:, there], st_sem.at[part_of])
                keep.start()
                stores.append(keep)

    end_gradients()
    for store in stores:
        store.wait()
    sent(a_all.at[pl.ds(0, 31)], a_send)
    sent(b_all.at[pl.ds(0, 14)], b_send)
    two = b_all.at[0, pl.ds(0, 256)]
    sent(two, b_last.at[0])
    pl.when(z < NZ - 1)(lambda: sent(two, b_last.at[1]))
    pl.when(z == 1)(lambda: sent(two, b_last.at[2]))
    sent(rs, rs_send)
    sent(hb_all.at[pl.ds(0, 2 * NC - 1)], hb_send)
    sent(up_send, up_sem.at[0])
    sent(pair_send, pair_sem.at[0])
    sent(grecv, g_send)
    sent(gbuf.at[h], gx_sem.at[0])
    for part_of in (0, 1):
        sent(stage.at[other, part_of], o_send.at[part_of])
        there = pl.ds(pl.multiple_of(other * 256 + part_of * 128, 128), 128)
        arrived(out.at[:, there], o_recv.at[part_of])


def write_out(merged, w, out, moments, merged_to, w_to, out_to, md, vd, mu, vu, merged_v, w_v, out_v, moments_v, sem):
    loads, stores = [], []
    for src, mid, dst in ((merged, merged_v, merged_to), (w, w_v, w_to), (out, out_v, out_to)):
        half = src.shape[0] // 2
        for rows in (pl.ds(0, half), pl.ds(half, half)):
            loads.append(pltpu.make_async_copy(src.at[rows], mid.at[rows], sem.at[len(loads)]))
            stores.append([pltpu.make_async_copy(mid.at[rows], dst.at[rows], sem.at[7 + len(stores)])])
    loads.append(pltpu.make_async_copy(moments, moments_v, sem.at[6]))
    stores.append([pltpu.make_async_copy(moments_v.at[i], ref, sem.at[13 + i]) for i, ref in enumerate((md, vd, mu, vu))])
    for load in loads:
        load.start()
    for load, after in zip(loads, stores):
        load.wait()
        for store in after:
            store.start()
    for after in stores:
        for store in after:
            store.wait()


def body(
    tokens, output_gradient, master_weight, old_down, old_up, fresh_down, fresh_up,
    m_down, v_down, m_up, v_up, keep_down, keep_up,
):
    dma = pltpu.SemaphoreType.DMA
    vmem = pltpu.VMEM
    hbm = pl.BlockSpec(memory_space=pltpu.HBM)
    results = pl.pallas_call(
        kernel,
        out_shape=(
            jax.ShapeDtypeStruct((512, 512), F32),
            jax.ShapeDtypeStruct((512, 512), BF16),
            jax.ShapeDtypeStruct((256, 512), BF16),
            jax.ShapeDtypeStruct((4, 32, 128), F32),
        ),
        in_specs=[hbm] * 13,
        out_specs=(hbm,) * 4,
        scratch_shapes=[
            vmem((2 * NC, 256, 512), BF16),
            vmem((NZ, 512, 256), BF16),
            vmem((256, 512), BF16),
            vmem((512, 512), F32),
            vmem((512, 512), F32),
            vmem((512, 512), BF16),
            vmem((4, 32, 128), F32),
            vmem((512, 128), F32),
            vmem((128, 512), F32),
            vmem((512, 128), F32),
            vmem((128, 512), F32),
            vmem((NC, 16, 256), F32),
            vmem((NC - 1, 16, 256), F32),
            vmem((2 * NC, 16, 256), BF16),
            vmem((NZ, 2, 16, 128), F32),
            vmem((NZ, 16, 128), BF16),
            vmem((NZ, 16, 128), BF16),
            vmem((2, NZ // 2, 2, 16, 128), F32),
            vmem((NZ // 2, 2, 16, 128), BF16),
            vmem((NZ // 2, 2, 16, 128), BF16),
            vmem((NZ // 2, 2, 16, 128), BF16),
            vmem((NZ // 2 - 1, 2, 16, 128), BF16),
            vmem((2, 2, 16, 128), F32),
            vmem((2, 256, 256), F32),
            vmem((2, 2, 256, 128), BF16),
            vmem((4, 32, 128), F32),
            pltpu.SMEM((2, 2), jnp.int32),
            dma((14,)),
            dma((5,)),
            dma,
            dma((2, 8, 4)),
            dma((2, 4)),
            dma((2, 4, 4)),
            dma((2, 4)),
            dma,
            dma,
            dma,
            dma,
            dma,
            dma((2,)),
            dma((2,)),
            dma,
            dma,
            dma((2,)),
            dma((2,)),
            dma((2,)),
            pltpu.SemaphoreType.REGULAR((3,)),
            dma((3,)),
        ],
        compiler_params=pltpu.CompilerParams(
            collective_id=0, has_side_effects=True, vmem_limit_bytes=60 * 1024 * 1024
        ),
        name="relora_step",
    )(
        tokens, output_gradient, master_weight, old_down, old_up, fresh_down, fresh_up,
        m_down, v_down, m_up.T, v_up.T, keep_down, keep_up,
    )
    small = jax.ShapeDtypeStruct((32, 128), F32)
    merged_weight, w_copy, outputs, md, vd, mu, vu = pl.pallas_call(
        write_out,
        out_shape=(
            jax.ShapeDtypeStruct((512, 512), F32),
            jax.ShapeDtypeStruct((512, 512), BF16),
            jax.ShapeDtypeStruct((256, 512), BF16),
            small, small, small, small,
        ),
        in_specs=[hbm] * 4,
        out_specs=(hbm,) * 7,
        scratch_shapes=[
            vmem((512, 512), F32), vmem((512, 512), BF16), vmem((256, 512), BF16), vmem((4, 32, 128), F32), dma((17,)),
        ],
        compiler_params=pltpu.CompilerParams(vmem_limit_bytes=60 * 1024 * 1024),
        name="write_out",
    )(*results)
    return (merged_weight, w_copy, outputs, md, vd, mu.T, vu.T)


def solution(mesh):
    both = P(("row", "rep"), "col")
    tile = P("row", "col")
    down = P(("col", "row"), None)
    up = P(None, ("col", "row"))
    flags = P(("col", "row"))
    return jax.shard_map(
        body,
        mesh=mesh,
        in_specs=(
            both, both, tile, P("row", None), P(None, "col"), P("col", None), P(None, "col"),
            down, down, up, up, flags, flags,
        ),
        out_specs=(tile, tile, both, down, down, up, up),
        check_vma=False,
    )
```
